32 devices in a mesh: dp: 4 (over y, x), row: 2 (over core), col: 4 (over z).
Axes of the slice: x: 2, y: 2, z: 4, core: 2. Of those that a mesh axis runs over, the one named last changes fastest.
Arguments:
- inputs: bfloat16 [4, 64, 128, 128], P('dp', 'row', 'col'), may hold values from -6 to 6
- cotangent: bfloat16 [4, 64, 128, 128], P('dp', 'row', 'col'), may hold values from -6 to 6
- first_kernel: bfloat16 [3, 384, 128], replicated, may hold values from -0.1875 to 0.1875
- second_kernel: bfloat16 [3, 384, 128], replicated, may hold values from -0.1875 to 0.1875
Outputs:
- output: bfloat16 [4, 64, 128, 128], P('dp', 'row', 'col')
- grad_one: float32 [3, 384, 128], P(None, ('row', 'col'), 'dp')
- grad_two: float32 [3, 384, 128], P(None, ('row', 'col'), 'dp')
The draws below stay inside these ranges and needn't reach their ends.
All inputs are finite; a program needn't handle non-finite values.
Results may differ from the reference program's by a relative error of at most 0.0095.
Values may be sent and summed in bfloat16 or wider, within the bound.
A program may use at most 64 MiB of HBM per device.

```python
import jax
import jax.numpy as jnp
from jax import lax

C = 128
DILATION_ONE = 64
DILATION_TWO = 128
SAMPLES = 4
NH = 64
NW = 128


def raised(array, rng, source, target, parts, factor):
    owner, partner = [(jnp.arange(array.shape[axis_at]) // (array.shape[axis_at] // parts)).reshape([-1 if axis == axis_at else 1 for axis in range(array.ndim)]) for axis_at in (source, target)]
    chosen = jax.random.permutation(rng, parts)[partner]
    strong = (owner == chosen) | (owner == (partner + parts // 2) % parts)
    return jnp.where(strong, factor * array, array)


def block_scale(rng, dims, cuts, smallest, top_value):
    def one(axis_at, shards_of):
        heights = jax.random.uniform(jax.random.fold_in(jax.random.fold_in(rng, 6), axis_at), (shards_of,), jnp.float32, smallest / len(cuts), top_value / len(cuts))
        return jnp.repeat(jnp.exp(heights), dims[axis_at] // shards_of).reshape((-1,) + (1,) * (len(dims) - axis_at - 1))

    level = one(*cuts[0])
    for cut in cuts[1:]:
        level = level * one(*cut)
    return level


def scatter_about(own_key, extent, width, bound, cuts=(), kind=jnp.bfloat16):
    factor_of = block_scale(own_key, extent, cuts, -0.22, 0.18) if cuts else 1.0
    drawn = jax.random.normal(own_key, extent, jnp.float32) * width * factor_of
    return jnp.minimum(jnp.maximum(drawn, -bound), bound).astype(kind)


def gaussian_with(stream_key, dims, scale, reach, split, heavy, dtype=jnp.bfloat16):
    entries = scale * jax.random.normal(stream_key, dims, jnp.float32)
    if split:
        entries = entries * block_scale(stream_key, dims, split, -0.22, 0.18)
    return jnp.clip(raised(entries, jax.random.fold_in(stream_key, 3), *heavy), -reach, reach).astype(dtype)


def setup_inputs(seed: int = 0) -> dict:
    seeds = jax.random.split(jax.random.key(seed), 5)
    return {
        "inputs": gaussian_with(seeds[0], (SAMPLES, NH, NW, C), 1.0, 6.0, ((0, 4), (1, 2), (2, 4)), (1, 3, 2, 2.0)),
        "cotangent": gaussian_with(seeds[1], (SAMPLES, NH, NW, C), 1.0, 6.0, ((0, 4), (1, 2), (2, 4)), (0, 3, 4, 2.0)),
        "first_kernel": scatter_about(seeds[2], (3, 3 * C, C), (9 * C) ** -0.5, 0.1875),
        "second_kernel": scatter_about(seeds[3], (3, 3 * C, C), (9 * C) ** -0.5, 0.1875),
    }


def silu_slope(value):
    sigma = jax.nn.sigmoid(value)
    return sigma * (1.0 + value * (1.0 - sigma))


def moved(input_grid, row_step, col_step):
    height, breadth = input_grid.shape[0], input_grid.shape[1]
    row_pad, col_pad = abs(row_step), abs(col_step)
    padded = jnp.pad(input_grid, ((row_pad, row_pad), (col_pad, col_pad), (0, 0)))
    return padded[row_pad + row_step:row_pad + row_step + height, col_pad + col_step:col_pad + col_step + breadth, :]


def stacked_taps(input_grid, row_off, dilation):
    return jnp.concatenate([moved(input_grid, row_off * dilation, col_off * dilation) for col_off in (-1, 0, 1)], axis=-1)


def apply_dilated_kernel(input_grid, weights, dilation):
    channels = input_grid.shape[-1]
    partial_terms = []
    for position, row_off in enumerate((-1, 0, 1)):
        stacked = stacked_taps(input_grid, row_off, dilation).reshape(-1, 3 * channels)
        partial_terms.append(jnp.dot(stacked, weights[position], preferred_element_type=jnp.float32).astype(jnp.bfloat16))
    summed = partial_terms[0].astype(jnp.float32) + partial_terms[1].astype(jnp.float32) + partial_terms[2].astype(jnp.float32)
    return summed.reshape(input_grid.shape)


def kernel_weight_gradient(input_grid, gradient, dilation):
    channels = input_grid.shape[-1]
    flat_grad = gradient.reshape(-1, channels)
    pieces = []
    for row_off in (-1, 0, 1):
        stacked = stacked_taps(input_grid, row_off, dilation).reshape(-1, 3 * channels)
        pieces.append(jnp.dot(stacked.T, flat_grad, preferred_element_type=jnp.float32))
    return jnp.stack(pieces)


def kernel_reversed_taps(weights):
    channels = weights.shape[2]
    return weights.reshape(3, 3, channels, channels)[::-1, ::-1].transpose(0, 1, 3, 2).reshape(3, 3 * channels, channels)


def reference(inputs, cotangent, first_kernel, second_kernel):
    def one_sample(sample_pair):
        input_grid, upstream = sample_pair
        first_conv_output = apply_dilated_kernel(input_grid, first_kernel, DILATION_ONE)
        hidden_activation = (input_grid.astype(jnp.float32) + jax.nn.silu(first_conv_output)).astype(jnp.bfloat16)
        second_conv_output = apply_dilated_kernel(hidden_activation, second_kernel, DILATION_TWO)
        output = (hidden_activation.astype(jnp.float32) + jax.nn.silu(second_conv_output)).astype(jnp.bfloat16)
        second_upstream_gradient = (upstream.astype(jnp.float32) * silu_slope(second_conv_output)).astype(jnp.bfloat16)
        backward_convolve = apply_dilated_kernel(second_upstream_gradient, kernel_reversed_taps(second_kernel), DILATION_TWO)
        grad_middle = (upstream.astype(jnp.float32) + backward_convolve).astype(jnp.bfloat16)
        first_upstream_gradient = (grad_middle.astype(jnp.float32) * silu_slope(first_conv_output)).astype(jnp.bfloat16)
        return output, kernel_weight_gradient(input_grid, first_upstream_gradient, DILATION_ONE), kernel_weight_gradient(hidden_activation, second_upstream_gradient, DILATION_TWO)

    output, firsts, seconds = lax.map(one_sample, (inputs, cotangent))
    return output, jnp.sum(firsts, axis=0), jnp.sum(seconds, axis=0)
```

```python
import functools

import jax
import jax.numpy as jnp
from jax import lax
from jax.experimental import pallas as pl
from jax.experimental.pallas import tpu as pltpu
from jax.sharding import PartitionSpec as P

DILATION_ONE = 64
DILATION_TWO = 128
MESH = pl.DeviceIdType.MESH
F32 = jnp.float32
BF16 = jnp.bfloat16


def passed_along(value, axis, steps):
    count = lax.axis_size(axis)
    first, last = (max(0, -steps), min(count, count - steps))
    return lax.ppermute(value, axis, [(source, source + steps) for source in range(first, last)])


def as_sent(x):

    def short(part):
        return part.astype(jnp.bfloat16) if part.dtype == jnp.float32 else part

    return jax.tree.map(short, x)


def silu_slope(value):
    sigma = jax.nn.sigmoid(value)
    return sigma * (1.0 + value * (1.0 - sigma))


def col_taps(input_grid, offset):
    shifted = []
    for sign_col in (-1, 1):
        if offset < lax.axis_size("col"):
            shifted.append(passed_along(input_grid, "col", -sign_col * offset))
        else:
            shifted.append(jnp.zeros_like(input_grid))
    return jnp.concatenate([shifted[0], input_grid, shifted[1]], axis=3)


def row_data(input_grid, by_tiles):
    if abs(by_tiles) < lax.axis_size("row"):
        return passed_along(as_sent(input_grid), "row", by_tiles).astype(input_grid.dtype)
    return jnp.zeros_like(input_grid)


def apply_dilated_kernel(input_grid, weights, dilation):
    offset = dilation // input_grid.shape[1]
    span_width = weights.shape[1]
    centre = col_taps(input_grid, offset)
    stacks = [row_data(centre, offset), centre, row_data(centre, -offset)]
    partial_terms = [
        jnp.dot(
            stacks[position].reshape(-1, span_width),
            weights[position],
            preferred_element_type=jnp.float32,
        ).astype(jnp.bfloat16)
        for position in range(3)
    ]
    summed = (
        partial_terms[0].astype(jnp.float32)
        + partial_terms[1].astype(jnp.float32)
        + partial_terms[2].astype(jnp.float32)
    )
    return (summed.reshape(input_grid.shape), stacks)


def kernel_weight_gradient(stacks, gradient):
    channels = gradient.shape[-1]
    span_width = 3 * channels
    contract = (((0,), (0,)), ((), ()))
    pieces = []
    flat_grad = gradient.reshape(-1, channels)
    for position in range(3):
        pieces.append(
            lax.dot_general(
                stacks[position].reshape(-1, span_width),
                flat_grad,
                contract,
                preferred_element_type=jnp.float32,
            )
        )
    return jnp.stack(pieces)


def kernel_reversed_taps(weights):
    channels = weights.shape[2]
    return (
        weights.reshape(3, 3, channels, channels)[::-1, ::-1]
        .transpose(0, 1, 3, 2)
        .reshape(3, 3 * channels, channels)
    )


def body(inputs, cotangent, first_kernel, second_kernel):
    first_conv_output, first_tap_stack = apply_dilated_kernel(inputs, first_kernel, DILATION_ONE)
    hidden_activation = (inputs.astype(jnp.float32) + jax.nn.silu(first_conv_output)).astype(
        jnp.bfloat16
    )
    second_conv_output, second_tap_stack = apply_dilated_kernel(
        hidden_activation, second_kernel, DILATION_TWO
    )
    output = (hidden_activation.astype(jnp.float32) + jax.nn.silu(second_conv_output)).astype(
        jnp.bfloat16
    )
    second_upstream_gradient = (
        cotangent.astype(jnp.float32) * silu_slope(second_conv_output)
    ).astype(jnp.bfloat16)
    backward_convolve, ignored_slot = apply_dilated_kernel(
        second_upstream_gradient, kernel_reversed_taps(second_kernel), DILATION_TWO
    )
    grad_second = kernel_weight_gradient(second_tap_stack, second_upstream_gradient)
    grad_middle = (cotangent.astype(jnp.float32) + backward_convolve).astype(jnp.bfloat16)
    first_upstream_gradient = (
        grad_middle.astype(jnp.float32) * silu_slope(first_conv_output)
    ).astype(jnp.bfloat16)
    grad_first = kernel_weight_gradient(first_tap_stack, first_upstream_gradient)
    tiles_summed = (
        lax.psum_scatter(grad_first, ("row", "col"), scatter_dimension=1, tiled=True),
        lax.psum_scatter(grad_second, ("row", "col"), scatter_dimension=1, tiled=True),
    )
    grad_one, grad_two = (
        lax.psum_scatter(tiles_summed[0], "dp", scatter_dimension=2, tiled=True),
        lax.psum_scatter(tiles_summed[1], "dp", scatter_dimension=2, tiled=True),
    )
    return (output, grad_one, grad_two)


def dot(a, b, contract):
    return lax.dot_general(a, b, (contract, ((), ())), preferred_element_type=F32)


def sigmoid(value):
    return 0.5 + 0.5 * jnp.tanh(0.5 * value)


def flipped(index, bits):
    bit = 1
    while bit <= bits:
        if bits & bit:
            index = index + bit - 2 * bit * lax.rem(lax.div(index, bit), 2)
        bit *= 2
    return index


def fused_kernel(
    sizes,
    x_hbm,
    cot_hbm,
    w1_hbm,
    w2_hbm,
    out,
    g1_ref,
    g2_ref,
    x,
    far,
    cot,
    w1,
    w2,
    acc,
    send1,
    recv1,
    send2,
    recv2,
    late_sem,
    load_sem,
    far_send,
    far_recv,
    share_send,
    share_recv,
    tile_send,
    tile_recv,
):
    samples, rows, cols, offset, chunk, window = sizes
    group = rows * cols
    cells, channels = x.shape
    chunks = cells // chunk
    shares = samples * rows
    share = channels // shares
    piece = 3 * channels // group
    my_dp = lax.axis_index("dp")
    my_row = lax.axis_index("row")
    my_col = lax.axis_index("col")
    me = my_row * cols + my_col
    low = my_col < offset
    partner = jnp.where(low, my_col + offset, my_col - offset)
    tap = jnp.where(low, 2 * channels, 0)
    inner = (my_col > 0) & (my_col < cols - 1)

    barrier = pltpu.get_barrier_semaphore()
    tile_peers = []
    for step in reversed(range(1, group)):
        col, row = flipped(my_col, step // rows), flipped(my_row, step % rows)
        tile_peers.append((row * cols + col, {"row": row, "col": col}))
    share_peers = []
    for step in range(samples):
        dp = jnp.where(step < my_dp, step, step + 1) if step < samples - 1 else my_dp
        for turn in reversed(range(rows)):
            row = flipped(my_row, turn)
            if step < samples - 1 or turn:
                share_peers.append((dp * rows + row, {"dp": dp, "row": row}))
    greeted = [({"row": flipped(my_row, turn)}, None) for turn in range(1, rows)]
    for step in range(rows, group):
        col = flipped(my_col, step // rows)
        where = {"row": flipped(my_row, step % rows), "col": col}
        if step == offset * rows:
            greeted.insert(0, (where, None))
        else:
            greeted.append((where, col > my_col))
    for step in range(rows, shares):
        dp = flipped(my_dp, step // rows)
        greeted.append(({"dp": dp, "row": flipped(my_row, step % rows)}, dp > my_dp))

    def greet(semaphore, where):
        pl.semaphore_signal(semaphore, inc=1, device_id=where, device_id_type=MESH)

    for where, later in greeted:
        if later is None:
            greet(barrier, where)
        else:
            pl.when(later)(functools.partial(greet, barrier, where))
    early = rows + (my_col + my_dp) * rows - jnp.where(low, 0, 1)
    late = (cols - 1 - my_col + samples - 1 - my_dp) * rows - jnp.where(low, 1, 0)

    loads = [
        pltpu.make_async_copy(x_hbm, x, load_sem.at[0]),
        pltpu.make_async_copy(
            w1_hbm.at[1, pl.ds(channels, channels)], w1.at[pl.ds(0, channels)], load_sem.at[1]
        ),
        pltpu.make_async_copy(
            w1_hbm.at[1, pl.ds(pl.multiple_of(tap, channels), channels)],
            w1.at[pl.ds(channels, channels)],
            load_sem.at[2],
        ),
        pltpu.make_async_copy(w2_hbm.at[1, pl.ds(channels, channels)], w2, load_sem.at[3]),
        pltpu.make_async_copy(cot_hbm, cot, load_sem.at[4]),
    ]
    for load in loads:
        load.start()
    g1_ref[...] = jnp.zeros_like(g1_ref)
    g2_ref[...] = jnp.zeros_like(g2_ref)
    acc[...] = jnp.zeros_like(acc)
    pl.semaphore_wait(barrier, early)

    def exchange(at):
        span = pl.ds(pl.multiple_of(at * chunk, chunk), chunk)
        return pltpu.make_async_remote_copy(
            src_ref=x_hbm.at[span],
            dst_ref=far.at[span],
            send_sem=far_send.at[at],
            recv_sem=far_recv.at[at],
            device_id={"col": partner},
            device_id_type=MESH,
        )

    first = jnp.where(inner, chunks, window)

    @pl.loop(0, first)
    def _(at):
        exchange(at).start()

    for where, later in greeted:
        if later is not None:
            pl.when(jnp.logical_not(later))(functools.partial(greet, late_sem, where))
    for load in loads:
        load.wait()

    @pl.loop(0, chunks)
    def _(at):
        exchange(at).wait_recv()

        @pl.when(at + first < chunks)
        def _():
            exchange(at + first).start()

        span = pl.ds(pl.multiple_of(at * chunk, chunk), chunk)
        here = x[span]
        both = jnp.concatenate([here, far[span]], axis=1)
        conv_one = dot(both, w1[...], ((1,), (0,))).astype(BF16).astype(F32)
        sigma_one = sigmoid(conv_one)
        middle = (here.astype(F32) + conv_one * sigma_one).astype(BF16)
        conv_two = dot(middle, w2[...], ((1,), (0,))).astype(BF16).astype(F32)
        sigma_two = sigmoid(conv_two)
        out[span] = (middle.astype(F32) + conv_two * sigma_two).astype(BF16)
        upstream = cot[span].astype(F32)
        delta_two = (upstream * (sigma_two * (1.0 + conv_two * (1.0 - sigma_two)))).astype(BF16)
        back = dot(delta_two, w2[...], ((1,), (1,))).astype(BF16).astype(F32)
        acc[:, 2 * channels :] += dot(delta_two, middle, ((0,), (0,)))
        grad_middle = (upstream + back).astype(BF16).astype(F32)
        delta_one = (grad_middle * (sigma_one * (1.0 + conv_one * (1.0 - sigma_one)))).astype(BF16)
        acc[:, : 2 * channels] += dot(delta_one, both, ((0,), (0,)))

    send1[...] = acc[...].astype(BF16).reshape(send1.shape)
    mine = my_dp * rows + my_row

    def summed(step, slot):
        peer, where = share_peers[step]
        return pltpu.make_async_remote_copy(
            src_ref=send1.at[peer],
            dst_ref=recv1.at[slot],
            send_sem=share_send.at[step],
            recv_sem=share_recv.at[slot],
            device_id=where,
            device_id_type=MESH,
        )

    @pl.when(late > 0)
    def _():
        pl.semaphore_wait(late_sem, late)

    for step in range(shares - 1):
        summed(step, mine).start()

    @pl.loop(0, chunks)
    def _(at):
        exchange(at).wait_send()

    total = send1[mine].astype(F32)
    for step in reversed(range(shares - 1)):
        peer = share_peers[step][0]
        summed(step, peer).wait_recv()
        total = total + recv1[peer].astype(F32)

    lane = lax.broadcasted_iota(jnp.int32, (share, channels), 1)

    def packed(peer):
        start = peer * piece
        shift = lax.rem(3 * channels - start, channels)
        place = start + lane
        back_place = place - piece
        centre = pltpu.roll(total[:, :channels], shift, 1)
        side = pltpu.roll(total[:, channels : 2 * channels], shift, 1)
        second = pltpu.roll(total[:, 2 * channels :], lax.rem(shift + piece, channels), 1)
        one = jnp.where((place >= tap) & (place < tap + channels), side, 0.0)
        one = jnp.where((place >= channels) & (place < 2 * channels), centre, one)
        two = jnp.where((back_place >= channels) & (back_place < 2 * channels), second, 0.0)
        return jnp.where(lane < piece, one, two).astype(BF16)

    pieces = []
    for step, (peer, where) in enumerate(tile_peers):
        send2[step] = packed(peer)
        pieces.append(
            pltpu.make_async_remote_copy(
                src_ref=send2.at[step],
                dst_ref=recv2.at[me],
                send_sem=tile_send.at[step],
                recv_sem=tile_recv.at[step],
                device_id=where,
                device_id_type=MESH,
            )
        )
        pieces[-1].start()
    recv2[me] = packed(me)
    for step in range(shares - 1):
        summed(step, mine).wait_send()
    for copy in pieces:
        copy.wait_send()
    for copy in pieces:
        copy.wait_recv()
    for part in range(rows):
        total = recv2[part * cols].astype(F32)
        for col in range(1, cols):
            total = total + recv2[part * cols + col].astype(F32)
        g1_ref[1, pl.ds(part * share, share)] = total[:, :piece]
        g2_ref[1, pl.ds(part * share, share)] = total[:, piece : 2 * piece]


def store_kernel(count, *refs):
    sems = refs[-1]
    copies = [
        pltpu.make_async_copy(refs[at], refs[count + at], sems.at[at]) for at in range(count)
    ]
    for copy in copies:
        copy.start()
    for copy in copies:
        copy.wait()


def fused_body(sizes, inputs, cotangent, first_kernel, second_kernel):
    samples, rows, cols, offset, chunk, window = sizes
    group = rows * cols
    channels = inputs.shape[-1]
    shares = samples * rows
    share = channels // shares
    piece = 3 * channels // group
    flat = (inputs.shape[1] * inputs.shape[2], channels)
    hbm = pl.BlockSpec(memory_space=pltpu.HBM)
    vmem = pl.BlockSpec(memory_space=pltpu.VMEM)
    dma = pltpu.SemaphoreType.DMA
    gradient = (3, channels // samples, piece)
    held = pl.pallas_call(
        functools.partial(fused_kernel, sizes),
        out_shape=(pltpu.VMEM(flat, BF16), pltpu.VMEM(gradient, F32), pltpu.VMEM(gradient, F32)),
        in_specs=[hbm] * 4,
        out_specs=(vmem, vmem, vmem),
        scratch_shapes=[
            pltpu.VMEM(flat, BF16),
            pltpu.VMEM(flat, BF16),
            pltpu.VMEM(flat, BF16),
            pltpu.VMEM((2 * channels, channels), BF16),
            pltpu.VMEM((channels, channels), BF16),
            pltpu.VMEM((channels, 3 * channels), F32),
            pltpu.VMEM((shares, share, 3 * channels), BF16),
            pltpu.VMEM((shares, share, 3 * channels), BF16),
            pltpu.VMEM((group - 1, share, channels), BF16),
            pltpu.VMEM((group, share, channels), BF16),
            pltpu.SemaphoreType.REGULAR,
            dma((5,)),
            dma((flat[0] // chunk,)),
            dma((flat[0] // chunk,)),
            dma((shares - 1,)),
            dma((shares,)),
            dma((group - 1,)),
            dma((group - 1,)),
        ],
        compiler_params=pltpu.CompilerParams(
            collective_id=0, has_side_effects=True, vmem_limit_bytes=16 * 1024 * 1024
        ),
    )(
        *(
            pltpu.with_memory_space_constraint(part, pltpu.HBM)
            for part in (
                inputs.reshape(flat),
                cotangent.reshape(flat),
                first_kernel,
                second_kernel,
            )
        )
    )
    output, grad_one, grad_two = pl.pallas_call(
        functools.partial(store_kernel, len(held)),
        out_shape=tuple(jax.ShapeDtypeStruct(part.shape, part.dtype) for part in held),
        in_specs=[pl.BlockSpec(memory_space=pl.ANY)] * len(held),
        out_specs=(hbm,) * len(held),
        scratch_shapes=[dma((len(held),))],
        compiler_params=pltpu.CompilerParams(vmem_limit_bytes=1024 * 1024),
    )(*held)
    return (output.reshape(inputs.shape), grad_one.swapaxes(1, 2), grad_two.swapaxes(1, 2))


def either_body(mesh, inputs, cotangent, first_kernel, second_kernel):
    samples, rows, cols = mesh.shape["dp"], mesh.shape["row"], mesh.shape["col"]
    _, height, width, channels = inputs.shape
    offset = DILATION_ONE // width
    piece = 3 * channels // (rows * cols)
    fits = (
        inputs.shape[0] == 1
        and samples > 1
        and all(count & (count - 1) == 0 for count in (samples, rows, cols))
        and DILATION_ONE >= rows * height
        and DILATION_TWO >= rows * height
        and DILATION_TWO >= cols * width
        and DILATION_ONE == offset * width
        and cols == 2 * offset
        and channels % 128 == 0
        and channels % (16 * samples * rows) == 0
        and 3 * channels % (rows * cols) == 0
        and 2 * piece <= channels
        and (height * width) % (2 * channels) == 0
        and height * width >= 4 * channels
    )
    if not fits:
        return body(inputs, cotangent, first_kernel, second_kernel)
    sizes = (samples, rows, cols, offset, 2 * channels, 2)
    return fused_body(sizes, inputs, cotangent, first_kernel, second_kernel)


def solution(mesh):
    placed = (P("dp", "row", "col", None), P("dp", "row", "col", None), P(), P())
    return jax.shard_map(
        functools.partial(either_body, mesh),
        mesh=mesh,
        in_specs=placed,
        out_specs=(
            P("dp", "row", "col", None),
            P(None, ("row", "col"), "dp"),
            P(None, ("row", "col"), "dp"),
        ),
        check_vma=False,
    )
```

```python
import functools

import jax
import jax.numpy as jnp
from jax import lax
from jax.experimental import pallas as pl
from jax.experimental.pallas import tpu as pltpu
from jax.sharding import PartitionSpec as P

DILATION_ONE = 64
DILATION_TWO = 128
MESH = pl.DeviceIdType.MESH
F32 = jnp.float32
BF16 = jnp.bfloat16


def passed_along(value, axis, steps):
    count = lax.axis_size(axis)
    first, last = (max(0, -steps), min(count, count - steps))
    return lax.ppermute(value, axis, [(source, source + steps) for source in range(first, last)])


def as_sent(x):

    def short(part):
        return part.astype(jnp.bfloat16) if part.dtype == jnp.float32 else part

    return jax.tree.map(short, x)


def silu_slope(value):
    sigma = jax.nn.sigmoid(value)
    return sigma * (1.0 + value * (1.0 - sigma))


def col_taps(input_grid, offset):
    shifted = []
    for sign_col in (-1, 1):
        if offset < lax.axis_size("col"):
            shifted.append(passed_along(input_grid, "col", -sign_col * offset))
        else:
            shifted.append(jnp.zeros_like(input_grid))
    return jnp.concatenate([shifted[0], input_grid, shifted[1]], axis=3)


def row_data(input_grid, by_tiles):
    if abs(by_tiles) < lax.axis_size("row"):
        return passed_along(as_sent(input_grid), "row", by_tiles).astype(input_grid.dtype)
    return jnp.zeros_like(input_grid)


def apply_dilated_kernel(input_grid, weights, dilation):
    offset = dilation // input_grid.shape[1]
    span_width = weights.shape[1]
    centre = col_taps(input_grid, offset)
    stacks = [row_data(centre, offset), centre, row_data(centre, -offset)]
    partial_terms = [
        jnp.dot(
            stacks[position].reshape(-1, span_width),
            weights[position],
            preferred_element_type=jnp.float32,
        ).astype(jnp.bfloat16)
        for position in range(3)
    ]
    summed = (
        partial_terms[0].astype(jnp.float32)
        + partial_terms[1].astype(jnp.float32)
        + partial_terms[2].astype(jnp.float32)
    )
    return (summed.reshape(input_grid.shape), stacks)


def kernel_weight_gradient(stacks, gradient):
    channels = gradient.shape[-1]
    span_width = 3 * channels
    contract = (((0,), (0,)), ((), ()))
    pieces = []
    flat_grad = gradient.reshape(-1, channels)
    for position in range(3):
        pieces.append(
            lax.dot_general(
                stacks[position].reshape(-1, span_width),
                flat_grad,
                contract,
                preferred_element_type=jnp.float32,
            )
        )
    return jnp.stack(pieces)


def kernel_reversed_taps(weights):
    channels = weights.shape[2]
    return (
        weights.reshape(3, 3, channels, channels)[::-1, ::-1]
        .transpose(0, 1, 3, 2)
        .reshape(3, 3 * channels, channels)
    )


def body(inputs, cotangent, first_kernel, second_kernel):
    first_conv_output, first_tap_stack = apply_dilated_kernel(inputs, first_kernel, DILATION_ONE)
    hidden_activation = (inputs.astype(jnp.float32) + jax.nn.silu(first_conv_output)).astype(
        jnp.bfloat16
    )
    second_conv_output, second_tap_stack = apply_dilated_kernel(
        hidden_activation, second_kernel, DILATION_TWO
    )
    output = (hidden_activation.astype(jnp.float32) + jax.nn.silu(second_conv_output)).astype(
        jnp.bfloat16
    )
    second_upstream_gradient = (
        cotangent.astype(jnp.float32) * silu_slope(second_conv_output)
    ).astype(jnp.bfloat16)
    backward_convolve, ignored_slot = apply_dilated_kernel(
        second_upstream_gradient, kernel_reversed_taps(second_kernel), DILATION_TWO
    )
    grad_second = kernel_weight_gradient(second_tap_stack, second_upstream_gradient)
    grad_middle = (cotangent.astype(jnp.float32) + backward_convolve).astype(jnp.bfloat16)
    first_upstream_gradient = (
        grad_middle.astype(jnp.float32) * silu_slope(first_conv_output)
    ).astype(jnp.bfloat16)
    grad_first = kernel_weight_gradient(first_tap_stack, first_upstream_gradient)
    tiles_summed = (
        lax.psum_scatter(grad_first, ("row", "col"), scatter_dimension=1, tiled=True),
        lax.psum_scatter(grad_second, ("row", "col"), scatter_dimension=1, tiled=True),
    )
    grad_one, grad_two = (
        lax.psum_scatter(tiles_summed[0], "dp", scatter_dimension=2, tiled=True),
        lax.psum_scatter(tiles_summed[1], "dp", scatter_dimension=2, tiled=True),
    )
    return (output, grad_one, grad_two)


def dot(a, b, contract):
    return lax.dot_general(a, b, (contract, ((), ())), preferred_element_type=F32)


def sigmoid(value):
    return 0.5 + 0.5 * jnp.tanh(0.5 * value)


def flipped(index, bits):
    bit = 1
    while bit <= bits:
        if bits & bit:
            index = index + bit - 2 * bit * lax.rem(lax.div(index, bit), 2)
        bit *= 2
    return index


def fused_kernel(
    sizes,
    x_hbm,
    cot_hbm,
    w1_hbm,
    w2_hbm,
    out,
    g1_ref,
    g2_ref,
    x,
    far,
    cot,
    w1,
    w2,
    acc,
    send1,
    recv1,
    send2,
    recv2,
    head_out,
    head_in,
    late_sem,
    load_sem,
    far_send,
    far_recv,
    share_send,
    share_recv,
    tile_send,
    tile_recv,
    head_send,
    head_recv,
):
    samples, rows, cols, offset, chunk = sizes
    group = rows * cols
    cells, channels = x.shape
    chunks = cells // chunk
    shares = samples * rows
    share = channels // shares
    piece = 3 * channels // group
    my_dp = lax.axis_index("dp")
    my_row = lax.axis_index("row")
    my_col = lax.axis_index("col")
    me = my_row * cols + my_col
    low = my_col < offset
    partner = jnp.where(low, my_col + offset, my_col - offset)
    tap = jnp.where(low, 2 * channels, 0)
    head = (my_dp == 0) & (my_col == 0)
    far_end = my_col == cols - 1

    barrier = pltpu.get_barrier_semaphore()
    tile_peers = []
    for step in reversed(range(1, group)):
        col, row = flipped(my_col, step // rows), flipped(my_row, step % rows)
        tile_peers.append((row * cols + col, {"row": row, "col": col}))
    share_peers = []
    for step in range(samples):
        dp = jnp.where(step < my_dp, step, step + 1) if step < samples - 1 else my_dp
        for turn in reversed(range(rows)):
            row = flipped(my_row, turn)
            if step < samples - 1 or turn:
                share_peers.append((dp * rows + row, {"dp": dp, "row": row}))
    greeted = [({"row": flipped(my_row, turn)}, None) for turn in range(1, rows)]
    for step in range(rows, group):
        col = flipped(my_col, step // rows)
        where = {"row": flipped(my_row, step % rows), "col": col}
        if step == offset * rows:
            greeted.insert(0, (where, None))
        else:
            greeted.append((where, col > my_col))
    for step in range(rows, shares):
        dp = flipped(my_dp, step // rows)
        greeted.append(({"dp": dp, "row": flipped(my_row, step % rows)}, dp > my_dp))

    def greet(semaphore, where):
        pl.semaphore_signal(semaphore, inc=1, device_id=where, device_id_type=MESH)

    for where, later in greeted:
        if later is None:
            greet(barrier, where)
        else:
            pl.when(later)(functools.partial(greet, barrier, where))

    @pl.when(head)
    def _():
        for dp in range(1, samples):
            for row in range(rows):
                greet(barrier, {"dp": dp, "row": row, "col": cols - 1})

    early = rows + (my_col + my_dp) * rows - jnp.where(low, 0, 1)
    early = early + jnp.where(far_end & (my_dp > 0), rows, 0)
    late = (cols - 1 - my_col + samples - 1 - my_dp) * rows - jnp.where(low, 1, 0)

    loads = [
        pltpu.make_async_copy(x_hbm, x, load_sem.at[0]),
        pltpu.make_async_copy(
            w1_hbm.at[1, pl.ds(channels, channels)], w1.at[pl.ds(0, channels)], load_sem.at[1]
        ),
        pltpu.make_async_copy(
            w1_hbm.at[1, pl.ds(pl.multiple_of(tap, channels), channels)],
            w1.at[pl.ds(channels, channels)],
            load_sem.at[2],
        ),
        pltpu.make_async_copy(w2_hbm.at[1, pl.ds(channels, channels)], w2, load_sem.at[3]),
        pltpu.make_async_copy(cot_hbm, cot, load_sem.at[4]),
    ]
    for load in loads:
        load.start()
    g1_ref[...] = jnp.zeros_like(g1_ref)
    g2_ref[...] = jnp.zeros_like(g2_ref)
    acc[...] = jnp.zeros_like(acc)
    pl.semaphore_wait(barrier, early)

    def exchange(at):
        span = pl.ds(pl.multiple_of(at * chunk, chunk), chunk)
        return pltpu.make_async_remote_copy(
            src_ref=x_hbm.at[span],
            dst_ref=far.at[span],
            send_sem=far_send.at[at],
            recv_sem=far_recv.at[at],
            device_id={"col": partner},
            device_id_type=MESH,
        )

    @pl.loop(0, chunks)
    def _(at):
        exchange(at).start()

    for where, later in greeted:
        if later is not None:
            pl.when(jnp.logical_not(later))(functools.partial(greet, late_sem, where))
    for load in loads:
        load.wait()

    @pl.loop(0, chunks)
    def _(at):
        exchange(at).wait_recv()
        span = pl.ds(pl.multiple_of(at * chunk, chunk), chunk)
        here = x[span]
        both = jnp.concatenate([here, far[span]], axis=1)
        conv_one = dot(both, w1[...], ((1,), (0,))).astype(BF16).astype(F32)
        sigma_one = sigmoid(conv_one)
        middle = (here.astype(F32) + conv_one * sigma_one).astype(BF16)
        conv_two = dot(middle, w2[...], ((1,), (0,))).astype(BF16).astype(F32)
        sigma_two = sigmoid(conv_two)
        out[span] = (middle.astype(F32) + conv_two * sigma_two).astype(BF16)
        upstream = cot[span].astype(F32)
        delta_two = (upstream * (sigma_two * (1.0 + conv_two * (1.0 - sigma_two)))).astype(BF16)
        back = dot(delta_two, w2[...], ((1,), (1,))).astype(BF16).astype(F32)
        acc[:, 2 * channels :] += dot(delta_two, middle, ((0,), (0,)))
        grad_middle = (upstream + back).astype(BF16).astype(F32)
        delta_one = (grad_middle * (sigma_one * (1.0 + conv_one * (1.0 - sigma_one)))).astype(BF16)
        acc[:, : 2 * channels] += dot(delta_one, both, ((0,), (0,)))

    def packed(total, peer):
        lane = lax.broadcasted_iota(jnp.int32, (total.shape[0], channels), 1)
        start = peer * piece
        shift = lax.rem(3 * channels - start, channels)
        place = start + lane
        back_place = place - piece
        centre = pltpu.roll(total[:, :channels], shift, 1)
        side = pltpu.roll(total[:, channels : 2 * channels], shift, 1)
        second = pltpu.roll(total[:, 2 * channels :], lax.rem(shift + piece, channels), 1)
        one = jnp.where((place >= tap) & (place < tap + channels), side, 0.0)
        one = jnp.where((place >= channels) & (place < 2 * channels), centre, one)
        two = jnp.where((back_place >= channels) & (back_place < 2 * channels), second, 0.0)
        return jnp.where(lane < piece, one, two).astype(BF16)

    def ahead(row, slot):
        return pltpu.make_async_remote_copy(
            src_ref=head_out.at[row],
            dst_ref=head_in.at[slot],
            send_sem=head_send.at[row],
            recv_sem=head_recv.at[slot],
            device_id={"dp": 0, "row": row, "col": 0},
            device_id_type=MESH,
        )

    mine = my_dp * rows + my_row

    @pl.when(far_end)
    def _():
        for row in range(rows):
            head_out[row] = packed(acc[: rows * share, :], row * cols)
            ahead(row, mine).start()

    send1[...] = acc[...].astype(BF16).reshape(send1.shape)

    def summed(step, slot):
        peer, where = share_peers[step]
        return pltpu.make_async_remote_copy(
            src_ref=send1.at[peer],
            dst_ref=recv1.at[slot],
            send_sem=share_send.at[step],
            recv_sem=share_recv.at[slot],
            device_id=where,
            device_id_type=MESH,
        )

    @pl.when(late > 0)
    def _():
        pl.semaphore_wait(late_sem, late)

    for step in range(shares - 1):
        summed(step, mine).start()

    @pl.loop(0, chunks)
    def _(at):
        exchange(at).wait_send()

    total = send1[mine].astype(F32)
    for step in reversed(range(shares - 1)):
        peer = share_peers[step][0]
        summed(step, peer).wait_recv()
        total = total + recv1[peer].astype(F32)

    pieces = []
    for step, (peer, where) in enumerate(tile_peers):
        used = jnp.logical_not(far_end & (my_dp == 0) & (where["col"] == 0))
        heard = jnp.logical_not(head & (where["col"] == cols - 1))
        copy = pltpu.make_async_remote_copy(
            src_ref=send2.at[step],
            dst_ref=recv2.at[me],
            send_sem=tile_send.at[step],
            recv_sem=tile_recv.at[step],
            device_id=where,
            device_id_type=MESH,
        )
        send2[step] = packed(total, peer)
        pl.when(used)(copy.start)
        pieces.append((copy, used, heard))
    recv2[me] = packed(total, me)
    for step in range(shares - 1):
        summed(step, mine).wait_send()
    for copy, used, _ in pieces:
        pl.when(used)(copy.wait_send)

    @pl.when(far_end)
    def _():
        for row in range(rows):
            ahead(row, mine).wait_send()

    for copy, _, heard in pieces:
        pl.when(heard)(copy.wait_recv)

    def finish(total, at, size):
        g1_ref[1, pl.ds(at, size)] = total[:, :piece]
        g2_ref[1, pl.ds(at, size)] = total[:, piece : 2 * piece]

    def gathered(part, count):
        total = recv2[part * cols].astype(F32)
        for col in range(1, count):
            total = total + recv2[part * cols + col].astype(F32)
        return total

    @pl.when(jnp.logical_not(head))
    def _():
        for part in range(rows):
            finish(gathered(part, cols), part * share, share)

    @pl.when(head)
    def _():
        total = jnp.concatenate([gathered(part, cols - 1) for part in range(rows)], axis=0)
        for slot in range(shares):
            ahead(0, slot).wait_recv()
            total = total + head_in[slot].astype(F32)
        finish(total, 0, rows * share)


def store_kernel(count, *refs):
    sems = refs[-1]
    copies = [
        pltpu.make_async_copy(refs[at], refs[count + at], sems.at[at]) for at in range(count)
    ]
    for copy in copies:
        copy.start()
    for copy in copies:
        copy.wait()


def fused_body(sizes, inputs, cotangent, first_kernel, second_kernel):
    samples, rows, cols, offset, chunk = sizes
    group = rows * cols
    channels = inputs.shape[-1]
    shares = samples * rows
    share = channels // shares
    piece = 3 * channels // group
    flat = (inputs.shape[1] * inputs.shape[2], channels)
    hbm = pl.BlockSpec(memory_space=pltpu.HBM)
    vmem = pl.BlockSpec(memory_space=pltpu.VMEM)
    dma = pltpu.SemaphoreType.DMA
    gradient = (3, channels // samples, piece)
    held = pl.pallas_call(
        functools.partial(fused_kernel, sizes),
        out_shape=(pltpu.VMEM(flat, BF16), pltpu.VMEM(gradient, F32), pltpu.VMEM(gradient, F32)),
        in_specs=[hbm] * 4,
        out_specs=(vmem, vmem, vmem),
        scratch_shapes=[
            pltpu.VMEM(flat, BF16),
            pltpu.VMEM(flat, BF16),
            pltpu.VMEM(flat, BF16),
            pltpu.VMEM((2 * channels, channels), BF16),
            pltpu.VMEM((channels, channels), BF16),
            pltpu.VMEM((channels, 3 * channels), F32),
            pltpu.VMEM((shares, share, 3 * channels), BF16),
            pltpu.VMEM((shares, share, 3 * channels), BF16),
            pltpu.VMEM((group - 1, share, channels), BF16),
            pltpu.VMEM((group, share, channels), BF16),
            pltpu.VMEM((rows, rows * share, channels), BF16),
            pltpu.VMEM((shares, rows * share, channels), BF16),
            pltpu.SemaphoreType.REGULAR,
            dma((5,)),
            dma((flat[0] // chunk,)),
            dma((flat[0] // chunk,)),
            dma((shares - 1,)),
            dma((shares,)),
            dma((group - 1,)),
            dma((group - 1,)),
            dma((rows,)),
            dma((shares,)),
        ],
        compiler_params=pltpu.CompilerParams(
            collective_id=0, has_side_effects=True, vmem_limit_bytes=16 * 1024 * 1024
        ),
    )(
        *(
            pltpu.with_memory_space_constraint(part, pltpu.HBM)
            for part in (
                inputs.reshape(flat),
                cotangent.reshape(flat),
                first_kernel,
                second_kernel,
            )
        )
    )
    output, grad_one, grad_two = pl.pallas_call(
        functools.partial(store_kernel, len(held)),
        out_shape=tuple(jax.ShapeDtypeStruct(part.shape, part.dtype) for part in held),
        in_specs=[pl.BlockSpec(memory_space=pl.ANY)] * len(held),
        out_specs=(hbm,) * len(held),
        scratch_shapes=[dma((len(held),))],
        compiler_params=pltpu.CompilerParams(vmem_limit_bytes=1024 * 1024),
    )(*held)
    return (output.reshape(inputs.shape), grad_one.swapaxes(1, 2), grad_two.swapaxes(1, 2))


def either_body(mesh, inputs, cotangent, first_kernel, second_kernel):
    samples, rows, cols = mesh.shape["dp"], mesh.shape["row"], mesh.shape["col"]
    _, height, width, channels = inputs.shape
    offset = DILATION_ONE // width
    piece = 3 * channels // (rows * cols)
    fits = (
        inputs.shape[0] == 1
        and samples > 1
        and all(count & (count - 1) == 0 for count in (samples, rows, cols))
        and DILATION_ONE >= rows * height
        and DILATION_TWO >= rows * height
        and DILATION_TWO >= cols * width
        and DILATION_ONE == offset * width
        and cols == 2 * offset
        and channels % 128 == 0
        and channels % (16 * samples * rows) == 0
        and 3 * channels % (rows * cols) == 0
        and 2 * piece <= channels
        and (height * width) % (2 * channels) == 0
        and height * width >= 4 * channels
    )
    if not fits:
        return body(inputs, cotangent, first_kernel, second_kernel)
    sizes = (samples, rows, cols, offset, 2 * channels)
    return fused_body(sizes, inputs, cotangent, first_kernel, second_kernel)


def solution(mesh):
    placed = (P("dp", "row", "col", None), P("dp", "row", "col", None), P(), P())
    return jax.shard_map(
        functools.partial(either_body, mesh),
        mesh=mesh,
        in_specs=placed,
        out_specs=(
            P("dp", "row", "col", None),
            P(None, ("row", "col"), "dp"),
            P(None, ("row", "col"), "dp"),
        ),
        check_vma=False,
    )
```

```python
import functools

import jax
import jax.numpy as jnp
from jax import lax
from jax.experimental import pallas as pl
from jax.experimental.pallas import tpu as pltpu
from jax.sharding import PartitionSpec as P

DILATION_ONE = 64
DILATION_TWO = 128
MESH = pl.DeviceIdType.MESH
F32 = jnp.float32
BF16 = jnp.bfloat16


def passed_along(value, axis, steps):
    count = lax.axis_size(axis)
    first, last = (max(0, -steps), min(count, count - steps))
    return lax.ppermute(value, axis, [(source, source + steps) for source in range(first, last)])


def as_sent(x):

    def short(part):
        return part.astype(jnp.bfloat16) if part.dtype == jnp.float32 else part

    return jax.tree.map(short, x)


def silu_slope(value):
    sigma = jax.nn.sigmoid(value)
    return sigma * (1.0 + value * (1.0 - sigma))


def col_taps(input_grid, offset):
    shifted = []
    for sign_col in (-1, 1):
        if offset < lax.axis_size("col"):
            shifted.append(passed_along(input_grid, "col", -sign_col * offset))
        else:
            shifted.append(jnp.zeros_like(input_grid))
    return jnp.concatenate([shifted[0], input_grid, shifted[1]], axis=3)


def row_data(input_grid, by_tiles):
    if abs(by_tiles) < lax.axis_size("row"):
        return passed_along(as_sent(input_grid), "row", by_tiles).astype(input_grid.dtype)
    return jnp.zeros_like(input_grid)


def apply_dilated_kernel(input_grid, weights, dilation):
    offset = dilation // input_grid.shape[1]
    span_width = weights.shape[1]
    centre = col_taps(input_grid, offset)
    stacks = [row_data(centre, offset), centre, row_data(centre, -offset)]
    partial_terms = [
        jnp.dot(
            stacks[position].reshape(-1, span_width),
            weights[position],
            preferred_element_type=jnp.float32,
        ).astype(jnp.bfloat16)
        for position in range(3)
    ]
    summed = (
        partial_terms[0].astype(jnp.float32)
        + partial_terms[1].astype(jnp.float32)
        + partial_terms[2].astype(jnp.float32)
    )
    return (summed.reshape(input_grid.shape), stacks)


def kernel_weight_gradient(stacks, gradient):
    channels = gradient.shape[-1]
    span_width = 3 * channels
    contract = (((0,), (0,)), ((), ()))
    pieces = []
    flat_grad = gradient.reshape(-1, channels)
    for position in range(3):
        pieces.append(
            lax.dot_general(
                stacks[position].reshape(-1, span_width),
                flat_grad,
                contract,
                preferred_element_type=jnp.float32,
            )
        )
    return jnp.stack(pieces)


def kernel_reversed_taps(weights):
    channels = weights.shape[2]
    return (
        weights.reshape(3, 3, channels, channels)[::-1, ::-1]
        .transpose(0, 1, 3, 2)
        .reshape(3, 3 * channels, channels)
    )


def body(inputs, cotangent, first_kernel, second_kernel):
    first_conv_output, first_tap_stack = apply_dilated_kernel(inputs, first_kernel, DILATION_ONE)
    hidden_activation = (inputs.astype(jnp.float32) + jax.nn.silu(first_conv_output)).astype(
        jnp.bfloat16
    )
    second_conv_output, second_tap_stack = apply_dilated_kernel(
        hidden_activation, second_kernel, DILATION_TWO
    )
    output = (hidden_activation.astype(jnp.float32) + jax.nn.silu(second_conv_output)).astype(
        jnp.bfloat16
    )
    second_upstream_gradient = (
        cotangent.astype(jnp.float32) * silu_slope(second_conv_output)
    ).astype(jnp.bfloat16)
    backward_convolve, ignored_slot = apply_dilated_kernel(
        second_upstream_gradient, kernel_reversed_taps(second_kernel), DILATION_TWO
    )
    grad_second = kernel_weight_gradient(second_tap_stack, second_upstream_gradient)
    grad_middle = (cotangent.astype(jnp.float32) + backward_convolve).astype(jnp.bfloat16)
    first_upstream_gradient = (
        grad_middle.astype(jnp.float32) * silu_slope(first_conv_output)
    ).astype(jnp.bfloat16)
    grad_first = kernel_weight_gradient(first_tap_stack, first_upstream_gradient)
    tiles_summed = (
        lax.psum_scatter(grad_first, ("row", "col"), scatter_dimension=1, tiled=True),
        lax.psum_scatter(grad_second, ("row", "col"), scatter_dimension=1, tiled=True),
    )
    grad_one, grad_two = (
        lax.psum_scatter(tiles_summed[0], "dp", scatter_dimension=2, tiled=True),
        lax.psum_scatter(tiles_summed[1], "dp", scatter_dimension=2, tiled=True),
    )
    return (output, grad_one, grad_two)


def dot(a, b, contract):
    return lax.dot_general(a, b, (contract, ((), ())), preferred_element_type=F32)


def sigmoid(value):
    return 0.5 + 0.5 * jnp.tanh(0.5 * value)


def flipped(index, bits):
    bit = 1
    while bit <= bits:
        if bits & bit:
            index = index + bit - 2 * bit * lax.rem(lax.div(index, bit), 2)
        bit *= 2
    return index


def fused_kernel(
    sizes,
    x_hbm,
    cot_hbm,
    w1_hbm,
    w2_hbm,
    out,
    g1_ref,
    g2_ref,
    x,
    far,
    cot,
    w1,
    w2,
    acc,
    send1,
    recv1,
    send2,
    recv2,
    head_out,
    head_in,
    late_sem,
    told_sem,
    load_sem,
    far_send,
    far_recv,
    share_send,
    share_recv,
    tile_send,
    tile_recv,
    head_send,
    head_recv,
):
    samples, rows, cols, offset, chunk, heads = sizes
    group = rows * cols
    cells, channels = x.shape
    chunks = cells // chunk
    shares = samples * rows
    share = channels // shares
    piece = 3 * channels // group
    my_dp = lax.axis_index("dp")
    my_row = lax.axis_index("row")
    my_col = lax.axis_index("col")
    me = my_row * cols + my_col
    low = my_col < offset
    partner = jnp.where(low, my_col + offset, my_col - offset)
    tap = jnp.where(low, 2 * channels, 0)
    far_end = my_col == cols - 1

    def is_head(dp, col):
        return functools.reduce(jnp.logical_or, [(dp == a) & (col == b) for a, b in heads])

    head = is_head(my_dp, my_col)

    barrier = pltpu.get_barrier_semaphore()
    tile_peers = []
    for step in reversed(range(1, group)):
        col, row = flipped(my_col, step // rows), flipped(my_row, step % rows)
        tile_peers.append((row * cols + col, {"row": row, "col": col}))
    share_peers = []
    for step in range(samples):
        dp = jnp.where(step < my_dp, step, step + 1) if step < samples - 1 else my_dp
        for turn in reversed(range(rows)):
            row = flipped(my_row, turn)
            if step < samples - 1 or turn:
                share_peers.append((dp * rows + row, {"dp": dp, "row": row}))
    replies = []
    greeted = [({"row": flipped(my_row, turn)}, None) for turn in range(1, rows)]
    for step in range(rows, group):
        col = flipped(my_col, step // rows)
        where = {"row": flipped(my_row, step % rows), "col": col}
        if step == offset * rows:
            greeted.insert(0, (where, None))
        else:
            greeted.append((where, col > my_col))
            replies.append((where, col < my_col))
    before, after = my_col, cols - 1 - my_col
    for mask in range(1, samples):
        dp = flipped(my_dp, mask)
        farther, nearer = dp - my_dp == mask, my_dp - dp == mask
        before = before + jnp.where(nearer, 1, 0)
        after = after + jnp.where(farther, 1, 0)
        for turn in range(rows):
            where = {"dp": dp, "row": flipped(my_row, turn)}
            greeted.append((where, farther))
            replies.append((where, nearer))
    told = [dp for dp in range(samples) if any(dp & other not in (dp, other) for other in range(samples))]

    def greet(semaphore, where):
        pl.semaphore_signal(semaphore, inc=1, device_id=where, device_id_type=MESH)

    for where, later in greeted:
        if later is None:
            greet(barrier, where)
        else:
            pl.when(later)(functools.partial(greet, barrier, where))

    @pl.when(head)
    def _():
        for step in range(rows, shares):
            where = {"dp": flipped(my_dp, step // rows), "row": flipped(my_row, step % rows)}
            greet(barrier, {**where, "col": cols - 1})

    early = rows + before * rows - jnp.where(low, 0, 1)
    for dp, _ in heads:
        early = early + jnp.where(far_end & (my_dp != dp), rows, 0)
    late = after * rows - jnp.where(low, 1, 0)

    loads = [
        pltpu.make_async_copy(x_hbm, x, load_sem.at[0]),
        pltpu.make_async_copy(
            w1_hbm.at[1, pl.ds(channels, channels)], w1.at[pl.ds(0, channels)], load_sem.at[1]
        ),
        pltpu.make_async_copy(
            w1_hbm.at[1, pl.ds(pl.multiple_of(tap, channels), channels)],
            w1.at[pl.ds(channels, channels)],
            load_sem.at[2],
        ),
        pltpu.make_async_copy(w2_hbm.at[1, pl.ds(channels, channels)], w2, load_sem.at[3]),
        pltpu.make_async_copy(cot_hbm, cot, load_sem.at[4]),
    ]
    for load in loads:
        load.start()
    g1_ref[...] = jnp.zeros_like(g1_ref)
    g2_ref[...] = jnp.zeros_like(g2_ref)
    acc[...] = jnp.zeros_like(acc)
    pl.semaphore_wait(barrier, early)

    def exchange(at):
        span = pl.ds(pl.multiple_of(at * chunk, chunk), chunk)
        return pltpu.make_async_remote_copy(
            src_ref=x_hbm.at[span],
            dst_ref=far.at[span],
            send_sem=far_send.at[at],
            recv_sem=far_recv.at[at],
            device_id={"col": partner},
            device_id_type=MESH,
        )

    @pl.loop(0, chunks)
    def _(at):
        exchange(at).start()

    for where, nearer in replies:
        pl.when(nearer)(functools.partial(greet, late_sem, where))
    for load in loads:
        load.wait()

    @pl.when(late > 0)
    def _():
        pl.semaphore_wait(late_sem, late)

    for dp in told:
        pl.when(my_dp == 0)(functools.partial(greet, told_sem, {"dp": dp}))
        pl.when(my_dp == dp)(functools.partial(pl.semaphore_wait, told_sem, 1))

    @pl.loop(0, chunks)
    def _(at):
        exchange(at).wait_recv()
        span = pl.ds(pl.multiple_of(at * chunk, chunk), chunk)
        here = x[span]
        both = jnp.concatenate([here, far[span]], axis=1)
        conv_one = dot(both, w1[...], ((1,), (0,))).astype(BF16).astype(F32)
        sigma_one = sigmoid(conv_one)
        middle = (here.astype(F32) + conv_one * sigma_one).astype(BF16)
        conv_two = dot(middle, w2[...], ((1,), (0,))).astype(BF16).astype(F32)
        sigma_two = sigmoid(conv_two)
        out[span] = (middle.astype(F32) + conv_two * sigma_two).astype(BF16)
        upstream = cot[span].astype(F32)
        delta_two = (upstream * (sigma_two * (1.0 + conv_two * (1.0 - sigma_two)))).astype(BF16)
        back = dot(delta_two, w2[...], ((1,), (1,))).astype(BF16).astype(F32)
        acc[:, 2 * channels :] += dot(delta_two, middle, ((0,), (0,)))
        grad_middle = (upstream + back).astype(BF16).astype(F32)
        delta_one = (grad_middle * (sigma_one * (1.0 + conv_one * (1.0 - sigma_one)))).astype(BF16)
        acc[:, : 2 * channels] += dot(delta_one, both, ((0,), (0,)))

    def packed(total, peer):
        lane = lax.broadcasted_iota(jnp.int32, (total.shape[0], channels), 1)
        start = peer * piece
        shift = lax.rem(3 * channels - start, channels)
        place = start + lane
        back_place = place - piece
        centre = pltpu.roll(total[:, :channels], shift, 1)
        side = pltpu.roll(total[:, channels : 2 * channels], shift, 1)
        second = pltpu.roll(total[:, 2 * channels :], lax.rem(shift + piece, channels), 1)
        one = jnp.where((place >= tap) & (place < tap + channels), side, 0.0)
        one = jnp.where((place >= channels) & (place < 2 * channels), centre, one)
        two = jnp.where((back_place >= channels) & (back_place < 2 * channels), second, 0.0)
        return jnp.where(lane < piece, one, two).astype(BF16)

    mine = my_dp * rows + my_row
    send1[...] = acc[...].astype(BF16).reshape(send1.shape)

    def summed(step, slot):
        peer, where = share_peers[step]
        return pltpu.make_async_remote_copy(
            src_ref=send1.at[peer],
            dst_ref=recv1.at[slot],
            send_sem=share_send.at[step],
            recv_sem=share_recv.at[slot],
            device_id=where,
            device_id_type=MESH,
        )

    for step in range(shares - 1):
        summed(step, mine).start()

    def ahead(at, slot):
        dp, col = heads[at // rows]
        return pltpu.make_async_remote_copy(
            src_ref=head_out.at[at],
            dst_ref=head_in.at[slot],
            send_sem=head_send.at[at],
            recv_sem=head_recv.at[slot],
            device_id={"dp": dp, "row": at % rows, "col": col},
            device_id_type=MESH,
        )

    @pl.when(far_end)
    def _():
        for at in range(len(heads) * rows):
            dp, col = heads[at // rows]
            lines = acc[dp * rows * share : (dp + 1) * rows * share, :]
            head_out[at] = packed(lines, at % rows * cols + col)
            ahead(at, mine).start()

    @pl.loop(0, chunks)
    def _(at):
        exchange(at).wait_send()

    total = send1[mine].astype(F32)
    for step in reversed(range(shares - 1)):
        peer = share_peers[step][0]
        summed(step, peer).wait_recv()
        total = total + recv1[peer].astype(F32)

    pieces = []
    for step, (peer, where) in enumerate(tile_peers):
        used = jnp.logical_not(far_end & is_head(my_dp, where["col"]))
        heard = jnp.logical_not(head & (where["col"] == cols - 1))
        copy = pltpu.make_async_remote_copy(
            src_ref=send2.at[step],
            dst_ref=recv2.at[me],
            send_sem=tile_send.at[step],
            recv_sem=tile_recv.at[step],
            device_id=where,
            device_id_type=MESH,
        )
        send2[step] = packed(total, peer)
        pl.when(used)(copy.start)
        pieces.append((copy, used, heard))
    recv2[me] = packed(total, me)
    for step in range(shares - 1):
        summed(step, mine).wait_send()
    for copy, used, _ in pieces:
        pl.when(used)(copy.wait_send)

    @pl.when(far_end)
    def _():
        for at in range(len(heads) * rows):
            ahead(at, mine).wait_send()

    for copy, _, heard in pieces:
        pl.when(heard)(copy.wait_recv)

    def finish(total, at, size):
        g1_ref[1, pl.ds(at, size)] = total[:, :piece]
        g2_ref[1, pl.ds(at, size)] = total[:, piece : 2 * piece]

    def gathered(part, count):
        total = recv2[part * cols].astype(F32)
        for col in range(1, count):
            total = total + recv2[part * cols + col].astype(F32)
        return total

    @pl.when(jnp.logical_not(head))
    def _():
        for part in range(rows):
            finish(gathered(part, cols), part * share, share)

    @pl.when(head)
    def _():
        total = jnp.concatenate([gathered(part, cols - 1) for part in range(rows)], axis=0)
        for slot in range(shares):
            ahead(0, slot).wait_recv()
            total = total + head_in[slot].astype(F32)
        finish(total, 0, rows * share)


def store_kernel(count, *refs):
    sems = refs[-1]
    copies = [
        pltpu.make_async_copy(refs[at], refs[count + at], sems.at[at]) for at in range(count)
    ]
    for copy in copies:
        copy.start()
    for copy in copies:
        copy.wait()


def fused_body(sizes, inputs, cotangent, first_kernel, second_kernel):
    samples, rows, cols, offset, chunk, heads = sizes
    group = rows * cols
    channels = inputs.shape[-1]
    shares = samples * rows
    share = channels // shares
    piece = 3 * channels // group
    flat = (inputs.shape[1] * inputs.shape[2], channels)
    hbm = pl.BlockSpec(memory_space=pltpu.HBM)
    vmem = pl.BlockSpec(memory_space=pltpu.VMEM)
    dma = pltpu.SemaphoreType.DMA
    gradient = (3, channels // samples, piece)
    held = pl.pallas_call(
        functools.partial(fused_kernel, sizes),
        out_shape=(pltpu.VMEM(flat, BF16), pltpu.VMEM(gradient, F32), pltpu.VMEM(gradient, F32)),
        in_specs=[hbm] * 4,
        out_specs=(vmem, vmem, vmem),
        scratch_shapes=[
            pltpu.VMEM(flat, BF16),
            pltpu.VMEM(flat, BF16),
            pltpu.VMEM(flat, BF16),
            pltpu.VMEM((2 * channels, channels), BF16),
            pltpu.VMEM((channels, channels), BF16),
            pltpu.VMEM((channels, 3 * channels), F32),
            pltpu.VMEM((shares, share, 3 * channels), BF16),
            pltpu.VMEM((shares, share, 3 * channels), BF16),
            pltpu.VMEM((group - 1, share, channels), BF16),
            pltpu.VMEM((group, share, channels), BF16),
            pltpu.VMEM((len(heads) * rows, rows * share, channels), BF16),
            pltpu.VMEM((shares, rows * share, channels), BF16),
            pltpu.SemaphoreType.REGULAR,
            pltpu.SemaphoreType.REGULAR,
            dma((5,)),
            dma((flat[0] // chunk,)),
            dma((flat[0] // chunk,)),
            dma((shares - 1,)),
            dma((shares,)),
            dma((group - 1,)),
            dma((group - 1,)),
            dma((len(heads) * rows,)),
            dma((shares,)),
        ],
        compiler_params=pltpu.CompilerParams(
            collective_id=0, has_side_effects=True, vmem_limit_bytes=16 * 1024 * 1024
        ),
    )(
        *(
            pltpu.with_memory_space_constraint(part, pltpu.HBM)
            for part in (
                inputs.reshape(flat),
                cotangent.reshape(flat),
                first_kernel,
                second_kernel,
            )
        )
    )
    output, grad_one, grad_two = pl.pallas_call(
        functools.partial(store_kernel, len(held)),
        out_shape=tuple(jax.ShapeDtypeStruct(part.shape, part.dtype) for part in held),
        in_specs=[pl.BlockSpec(memory_space=pl.ANY)] * len(held),
        out_specs=(hbm,) * len(held),
        scratch_shapes=[dma((len(held),))],
        compiler_params=pltpu.CompilerParams(vmem_limit_bytes=1024 * 1024),
    )(*held)
    return (output.reshape(inputs.shape), grad_one.swapaxes(1, 2), grad_two.swapaxes(1, 2))


def either_body(mesh, inputs, cotangent, first_kernel, second_kernel):
    samples, rows, cols = mesh.shape["dp"], mesh.shape["row"], mesh.shape["col"]
    _, height, width, channels = inputs.shape
    offset = DILATION_ONE // width
    piece = 3 * channels // (rows * cols)
    fits = (
        inputs.shape[0] == 1
        and samples > 1
        and all(count & (count - 1) == 0 for count in (samples, rows, cols))
        and DILATION_ONE >= rows * height
        and DILATION_TWO >= rows * height
        and DILATION_TWO >= cols * width
        and DILATION_ONE == offset * width
        and cols == 2 * offset
        and channels % 128 == 0
        and channels % (16 * samples * rows) == 0
        and 3 * channels % (rows * cols) == 0
        and 2 * piece <= channels
        and (height * width) % (2 * channels) == 0
        and height * width >= 4 * channels
    )
    if not fits:
        return body(inputs, cotangent, first_kernel, second_kernel)
    heads = [(0, 0)] + [(dp, 0) for dp in range(1, samples - 1)]
    if cols > 2:
        heads.append((0, 1))
    sizes = (samples, rows, cols, offset, 2 * channels, heads)
    return fused_body(sizes, inputs, cotangent, first_kernel, second_kernel)


def solution(mesh):
    placed = (P("dp", "row", "col", None), P("dp", "row", "col", None), P(), P())
    return jax.shard_map(
        functools.partial(either_body, mesh),
        mesh=mesh,
        in_specs=placed,
        out_specs=(
            P("dp", "row", "col", None),
            P(None, ("row", "col"), "dp"),
            P(None, ("row", "col"), "dp"),
        ),
        check_vma=False,
    )
```

```python
import functools

import jax
import jax.numpy as jnp
from jax import lax
from jax.experimental import pallas as pl
from jax.experimental.pallas import tpu as pltpu
from jax.sharding import PartitionSpec as P

DILATION_ONE = 64
DILATION_TWO = 128
MESH = pl.DeviceIdType.MESH
F32 = jnp.float32
BF16 = jnp.bfloat16


def passed_along(value, axis, steps):
    count = lax.axis_size(axis)
    first, last = (max(0, -steps), min(count, count - steps))
    return lax.ppermute(value, axis, [(source, source + steps) for source in range(first, last)])


def as_sent(x):

    def short(part):
        return part.astype(jnp.bfloat16) if part.dtype == jnp.float32 else part

    return jax.tree.map(short, x)


def silu_slope(value):
    sigma = jax.nn.sigmoid(value)
    return sigma * (1.0 + value * (1.0 - sigma))


def col_taps(input_grid, offset):
    shifted = []
    for sign_col in (-1, 1):
        if offset < lax.axis_size("col"):
            shifted.append(passed_along(input_grid, "col", -sign_col * offset))
        else:
            shifted.append(jnp.zeros_like(input_grid))
    return jnp.concatenate([shifted[0], input_grid, shifted[1]], axis=3)


def row_data(input_grid, by_tiles):
    if abs(by_tiles) < lax.axis_size("row"):
        return passed_along(as_sent(input_grid), "row", by_tiles).astype(input_grid.dtype)
    return jnp.zeros_like(input_grid)


def apply_dilated_kernel(input_grid, weights, dilation):
    offset = dilation // input_grid.shape[1]
    span_width = weights.shape[1]
    centre = col_taps(input_grid, offset)
    stacks = [row_data(centre, offset), centre, row_data(centre, -offset)]
    partial_terms = [
        jnp.dot(
            stacks[position].reshape(-1, span_width),
            weights[position],
            preferred_element_type=jnp.float32,
        ).astype(jnp.bfloat16)
        for position in range(3)
    ]
    summed = (
        partial_terms[0].astype(jnp.float32)
        + partial_terms[1].astype(jnp.float32)
        + partial_terms[2].astype(jnp.float32)
    )
    return (summed.reshape(input_grid.shape), stacks)


def kernel_weight_gradient(stacks, gradient):
    channels = gradient.shape[-1]
    span_width = 3 * channels
    contract = (((0,), (0,)), ((), ()))
    pieces = []
    flat_grad = gradient.reshape(-1, channels)
    for position in range(3):
        pieces.append(
            lax.dot_general(
                stacks[position].reshape(-1, span_width),
                flat_grad,
                contract,
                preferred_element_type=jnp.float32,
            )
        )
    return jnp.stack(pieces)


def kernel_reversed_taps(weights):
    channels = weights.shape[2]
    return (
        weights.reshape(3, 3, channels, channels)[::-1, ::-1]
        .transpose(0, 1, 3, 2)
        .reshape(3, 3 * channels, channels)
    )


def body(inputs, cotangent, first_kernel, second_kernel):
    first_conv_output, first_tap_stack = apply_dilated_kernel(inputs, first_kernel, DILATION_ONE)
    hidden_activation = (inputs.astype(jnp.float32) + jax.nn.silu(first_conv_output)).astype(
        jnp.bfloat16
    )
    second_conv_output, second_tap_stack = apply_dilated_kernel(
        hidden_activation, second_kernel, DILATION_TWO
    )
    output = (hidden_activation.astype(jnp.float32) + jax.nn.silu(second_conv_output)).astype(
        jnp.bfloat16
    )
    second_upstream_gradient = (
        cotangent.astype(jnp.float32) * silu_slope(second_conv_output)
    ).astype(jnp.bfloat16)
    backward_convolve, ignored_slot = apply_dilated_kernel(
        second_upstream_gradient, kernel_reversed_taps(second_kernel), DILATION_TWO
    )
    grad_second = kernel_weight_gradient(second_tap_stack, second_upstream_gradient)
    grad_middle = (cotangent.astype(jnp.float32) + backward_convolve).astype(jnp.bfloat16)
    first_upstream_gradient = (
        grad_middle.astype(jnp.float32) * silu_slope(first_conv_output)
    ).astype(jnp.bfloat16)
    grad_first = kernel_weight_gradient(first_tap_stack, first_upstream_gradient)
    tiles_summed = (
        lax.psum_scatter(grad_first, ("row", "col"), scatter_dimension=1, tiled=True),
        lax.psum_scatter(grad_second, ("row", "col"), scatter_dimension=1, tiled=True),
    )
    grad_one, grad_two = (
        lax.psum_scatter(tiles_summed[0], "dp", scatter_dimension=2, tiled=True),
        lax.psum_scatter(tiles_summed[1], "dp", scatter_dimension=2, tiled=True),
    )
    return (output, grad_one, grad_two)


def dot(a, b, contract):
    return lax.dot_general(a, b, (contract, ((), ())), preferred_element_type=F32)


def sigmoid(value):
    return 0.5 + 0.5 * jnp.tanh(0.5 * value)


def flipped(index, bits):
    bit = 1
    while bit <= bits:
        if bits & bit:
            index = index + bit - 2 * bit * lax.rem(lax.div(index, bit), 2)
        bit *= 2
    return index


def fused_kernel(
    sizes,
    x_hbm,
    cot_hbm,
    w1_hbm,
    w2_hbm,
    out,
    g1_ref,
    g2_ref,
    x,
    far,
    cot,
    w1,
    w2,
    acc,
    send1,
    recv1,
    send2,
    recv2,
    head_out,
    head_in,
    late_sem,
    told_sem,
    go_sem,
    load_sem,
    far_send,
    far_recv,
    share_send,
    share_recv,
    tile_send,
    tile_recv,
    head_send,
    head_recv,
):
    samples, rows, cols, offset, chunk, heads = sizes
    group = rows * cols
    cells, channels = x.shape
    chunks = cells // chunk
    shares = samples * rows
    share = channels // shares
    piece = 3 * channels // group
    my_dp = lax.axis_index("dp")
    my_row = lax.axis_index("row")
    my_col = lax.axis_index("col")
    me = my_row * cols + my_col
    low = my_col < offset
    partner = jnp.where(low, my_col + offset, my_col - offset)
    tap = jnp.where(low, 2 * channels, 0)
    last_col = offset
    far_end = my_col == last_col

    def is_head(dp, col):
        return functools.reduce(jnp.logical_or, [(dp == a) & (col == b) for a, b in heads])

    head = is_head(my_dp, my_col)

    barrier = pltpu.get_barrier_semaphore()
    tile_peers = []
    for step in reversed(range(1, group)):
        col, row = flipped(my_col, step // rows), flipped(my_row, step % rows)
        tile_peers.append((row * cols + col, {"row": row, "col": col}))
    share_peers = []
    for step in range(samples):
        dp = jnp.where(step < my_dp, step, step + 1) if step < samples - 1 else my_dp
        for turn in reversed(range(rows)):
            row = flipped(my_row, turn)
            if step < samples - 1 or turn:
                share_peers.append((dp * rows + row, {"dp": dp, "row": row}))

    def greet(semaphore, where):
        pl.semaphore_signal(semaphore, inc=1, device_id=where, device_id_type=MESH)

    def greet_plane(semaphore):
        for step in reversed(range(1, shares)):
            dp, row = flipped(my_dp, step // rows), flipped(my_row, step % rows)
            greet(semaphore, {"dp": dp, "row": row})

    front = my_col == 0
    greet(barrier, {"col": partner})

    @pl.when(front)
    def _():
        for col in reversed(range(1, cols)):
            if col != offset:
                greet(barrier, {"col": col})
        greet_plane(barrier)

    early = jnp.where(front, shares, jnp.where(my_col == offset, 1, 2))
    loads = [
        pltpu.make_async_copy(x_hbm, x, load_sem.at[0]),
        pltpu.make_async_copy(
            w1_hbm.at[1, pl.ds(channels, channels)], w1.at[pl.ds(0, channels)], load_sem.at[1]
        ),
        pltpu.make_async_copy(
            w1_hbm.at[1, pl.ds(pl.multiple_of(tap, channels), channels)],
            w1.at[pl.ds(channels, channels)],
            load_sem.at[2],
        ),
        pltpu.make_async_copy(w2_hbm.at[1, pl.ds(channels, channels)], w2, load_sem.at[3]),
        pltpu.make_async_copy(cot_hbm, cot, load_sem.at[4]),
    ]
    for load in loads:
        load.start()
    g1_ref[...] = jnp.zeros_like(g1_ref)
    g2_ref[...] = jnp.zeros_like(g2_ref)
    acc[...] = jnp.zeros_like(acc)
    pl.semaphore_wait(barrier, early)

    def exchange(at):
        span = pl.ds(pl.multiple_of(at * chunk, chunk), chunk)
        return pltpu.make_async_remote_copy(
            src_ref=x_hbm.at[span],
            dst_ref=far.at[span],
            send_sem=far_send.at[at],
            recv_sem=far_recv.at[at],
            device_id={"col": partner},
            device_id_type=MESH,
        )

    held = jnp.where(front, chunks - 1, 0) if cols == 4 else 0

    @pl.loop(0, chunks - held)
    def _(at):
        exchange(at).start()

    for load in loads:
        load.wait()

    @pl.when(front)
    def _():
        pl.semaphore_wait(late_sem, cols - 1)
        greet_plane(told_sem)
        pl.semaphore_wait(told_sem, shares - 1)
        for col in reversed(range(1, cols)):
            greet(late_sem, {"col": col})
        if cols == 4:
            pl.semaphore_wait(go_sem, 1)

    @pl.when(jnp.logical_not(front))
    def _():
        greet(late_sem, {"col": 0})

    @pl.loop(chunks - held, chunks)
    def _(at):
        exchange(at).start()

    @pl.loop(0, chunks)
    def _(at):
        exchange(at).wait_recv()

        if cols == 4:
            pl.when((my_col == 1) & (at == chunks - 1))(functools.partial(greet, go_sem, {"col": 0}))

        span = pl.ds(pl.multiple_of(at * chunk, chunk), chunk)
        here = x[span]
        both = jnp.concatenate([here, far[span]], axis=1)
        conv_one = dot(both, w1[...], ((1,), (0,))).astype(BF16).astype(F32)
        sigma_one = sigmoid(conv_one)
        middle = (here.astype(F32) + conv_one * sigma_one).astype(BF16)
        conv_two = dot(middle, w2[...], ((1,), (0,))).astype(BF16).astype(F32)
        sigma_two = sigmoid(conv_two)
        out[span] = (middle.astype(F32) + conv_two * sigma_two).astype(BF16)
        upstream = cot[span].astype(F32)
        delta_two = (upstream * (sigma_two * (1.0 + conv_two * (1.0 - sigma_two)))).astype(BF16)
        back = dot(delta_two, w2[...], ((1,), (1,))).astype(BF16).astype(F32)
        acc[:, 2 * channels :] += dot(delta_two, middle, ((0,), (0,)))
        grad_middle = (upstream + back).astype(BF16).astype(F32)
        delta_one = (grad_middle * (sigma_one * (1.0 + conv_one * (1.0 - sigma_one)))).astype(BF16)
        acc[:, : 2 * channels] += dot(delta_one, both, ((0,), (0,)))

    def packed(total, peer):
        lane = lax.broadcasted_iota(jnp.int32, (total.shape[0], channels), 1)
        start = peer * piece
        shift = lax.rem(3 * channels - start, channels)
        place = start + lane
        back_place = place - piece
        centre = pltpu.roll(total[:, :channels], shift, 1)
        side = pltpu.roll(total[:, channels : 2 * channels], shift, 1)
        second = pltpu.roll(total[:, 2 * channels :], lax.rem(shift + piece, channels), 1)
        one = jnp.where((place >= tap) & (place < tap + channels), side, 0.0)
        one = jnp.where((place >= channels) & (place < 2 * channels), centre, one)
        two = jnp.where((back_place >= channels) & (back_place < 2 * channels), second, 0.0)
        return jnp.where(lane < piece, one, two).astype(BF16)

    mine = my_dp * rows + my_row
    @pl.when(jnp.logical_not(front))
    def _():
        pl.semaphore_wait(late_sem, 1)

    def ahead(at, slot):
        dp, col = heads[at // rows]
        return pltpu.make_async_remote_copy(
            src_ref=head_out.at[at],
            dst_ref=head_in.at[slot],
            send_sem=head_send.at[at],
            recv_sem=head_recv.at[slot],
            device_id={"dp": dp, "row": at % rows, "col": col},
            device_id_type=MESH,
        )

    def send_ahead(ats):
        for at in ats:
            dp, col = heads[at // rows]
            lines = acc[dp * rows * share : (dp + 1) * rows * share, :]
            head_out[at] = packed(lines, at % rows * cols + col)
            ahead(at, mine).start()

    pl.when(far_end)(functools.partial(send_ahead, range(rows)))
    send1[...] = acc[...].astype(BF16).reshape(send1.shape)

    def summed(step, slot):
        peer, where = share_peers[step]
        return pltpu.make_async_remote_copy(
            src_ref=send1.at[peer],
            dst_ref=recv1.at[slot],
            send_sem=share_send.at[step],
            recv_sem=share_recv.at[slot],
            device_id=where,
            device_id_type=MESH,
        )

    for step in range(shares - 1):
        summed(step, mine).start()

    pl.when(far_end)(functools.partial(send_ahead, range(rows, len(heads) * rows)))

    @pl.loop(0, chunks)
    def _(at):
        exchange(at).wait_send()

    total = send1[mine].astype(F32)
    for step in reversed(range(shares - 1)):
        peer = share_peers[step][0]
        summed(step, peer).wait_recv()
        total = total + recv1[peer].astype(F32)

    pieces = []
    for step, (peer, where) in enumerate(tile_peers):
        used = jnp.logical_not(far_end & is_head(my_dp, where["col"]))
        heard = jnp.logical_not(head & (where["col"] == last_col))
        copy = pltpu.make_async_remote_copy(
            src_ref=send2.at[step],
            dst_ref=recv2.at[me],
            send_sem=tile_send.at[step],
            recv_sem=tile_recv.at[step],
            device_id=where,
            device_id_type=MESH,
        )
        send2[step] = packed(total, peer)
        pl.when(used)(copy.start)
        pieces.append((copy, used, heard))
    recv2[me] = packed(total, me)
    for step in range(shares - 1):
        summed(step, mine).wait_send()
    for copy, used, _ in pieces:
        pl.when(used)(copy.wait_send)

    @pl.when(far_end)
    def _():
        for at in range(len(heads) * rows):
            ahead(at, mine).wait_send()

    for copy, _, heard in pieces:
        pl.when(heard)(copy.wait_recv)

    def finish(total, at, size):
        g1_ref[1, pl.ds(at, size)] = total[:, :piece]
        g2_ref[1, pl.ds(at, size)] = total[:, piece : 2 * piece]

    def gathered(part, skip=None):
        used = [recv2[part * cols + col].astype(F32) for col in range(cols) if col != skip]
        return functools.reduce(jnp.add, used)

    @pl.when(jnp.logical_not(head))
    def _():
        for part in range(rows):
            finish(gathered(part), part * share, share)

    @pl.when(head)
    def _():
        total = jnp.concatenate([gathered(part, last_col) for part in range(rows)], axis=0)
        for slot in range(shares):
            ahead(0, slot).wait_recv()
            total = total + head_in[slot].astype(F32)
        finish(total, 0, rows * share)


def store_kernel(count, *refs):
    sems = refs[-1]
    copies = [
        pltpu.make_async_copy(refs[at], refs[count + at], sems.at[at]) for at in range(count)
    ]
    for copy in copies:
        copy.start()
    for copy in copies:
        copy.wait()


def fused_body(sizes, inputs, cotangent, first_kernel, second_kernel):
    samples, rows, cols, offset, chunk, heads = sizes
    group = rows * cols
    channels = inputs.shape[-1]
    shares = samples * rows
    share = channels // shares
    piece = 3 * channels // group
    flat = (inputs.shape[1] * inputs.shape[2], channels)
    hbm = pl.BlockSpec(memory_space=pltpu.HBM)
    vmem = pl.BlockSpec(memory_space=pltpu.VMEM)
    dma = pltpu.SemaphoreType.DMA
    gradient = (3, channels // samples, piece)
    held = pl.pallas_call(
        functools.partial(fused_kernel, sizes),
        out_shape=(pltpu.VMEM(flat, BF16), pltpu.VMEM(gradient, F32), pltpu.VMEM(gradient, F32)),
        in_specs=[hbm] * 4,
        out_specs=(vmem, vmem, vmem),
        scratch_shapes=[
            pltpu.VMEM(flat, BF16),
            pltpu.VMEM(flat, BF16),
            pltpu.VMEM(flat, BF16),
            pltpu.VMEM((2 * channels, channels), BF16),
            pltpu.VMEM((channels, channels), BF16),
            pltpu.VMEM((channels, 3 * channels), F32),
            pltpu.VMEM((shares, share, 3 * channels), BF16),
            pltpu.VMEM((shares, share, 3 * channels), BF16),
            pltpu.VMEM((group - 1, share, channels), BF16),
            pltpu.VMEM((group, share, channels), BF16),
            pltpu.VMEM((len(heads) * rows, rows * share, channels), BF16),
            pltpu.VMEM((shares, rows * share, channels), BF16),
            pltpu.SemaphoreType.REGULAR,
            pltpu.SemaphoreType.REGULAR,
            pltpu.SemaphoreType.REGULAR,
            dma((5,)),
            dma((flat[0] // chunk,)),
            dma((flat[0] // chunk,)),
            dma((shares - 1,)),
            dma((shares,)),
            dma((group - 1,)),
            dma((group - 1,)),
            dma((len(heads) * rows,)),
            dma((shares,)),
        ],
        compiler_params=pltpu.CompilerParams(
            collective_id=0, has_side_effects=True, vmem_limit_bytes=16 * 1024 * 1024
        ),
    )(
        *(
            pltpu.with_memory_space_constraint(part, pltpu.HBM)
            for part in (
                inputs.reshape(flat),
                cotangent.reshape(flat),
                first_kernel,
                second_kernel,
            )
        )
    )
    output, grad_one, grad_two = pl.pallas_call(
        functools.partial(store_kernel, len(held)),
        out_shape=tuple(jax.ShapeDtypeStruct(part.shape, part.dtype) for part in held),
        in_specs=[pl.BlockSpec(memory_space=pl.ANY)] * len(held),
        out_specs=(hbm,) * len(held),
        scratch_shapes=[dma((len(held),))],
        compiler_params=pltpu.CompilerParams(vmem_limit_bytes=1024 * 1024),
    )(*held)
    return (output.reshape(inputs.shape), grad_one.swapaxes(1, 2), grad_two.swapaxes(1, 2))


def either_body(mesh, inputs, cotangent, first_kernel, second_kernel):
    samples, rows, cols = mesh.shape["dp"], mesh.shape["row"], mesh.shape["col"]
    _, height, width, channels = inputs.shape
    offset = DILATION_ONE // width
    piece = 3 * channels // (rows * cols)
    fits = (
        inputs.shape[0] == 1
        and samples > 1
        and all(count & (count - 1) == 0 for count in (samples, rows, cols))
        and DILATION_ONE >= rows * height
        and DILATION_TWO >= rows * height
        and DILATION_TWO >= cols * width
        and DILATION_ONE == offset * width
        and cols == 2 * offset
        and channels % 128 == 0
        and channels % (16 * samples * rows) == 0
        and 3 * channels % (rows * cols) == 0
        and 2 * piece <= channels
        and (height * width) % (2 * channels) == 0
        and height * width >= 4 * channels
    )
    if not fits:
        return body(inputs, cotangent, first_kernel, second_kernel)
    heads = [(0, 0)] + [(dp, 0) for dp in range(1, samples - 1)]
    if cols > 2:
        heads.append((0, 1))
    sizes = (samples, rows, cols, offset, 2 * channels, heads)
    return fused_body(sizes, inputs, cotangent, first_kernel, second_kernel)


def solution(mesh):
    placed = (P("dp", "row", "col", None), P("dp", "row", "col", None), P(), P())
    return jax.shard_map(
        functools.partial(either_body, mesh),
        mesh=mesh,
        in_specs=placed,
        out_specs=(
            P("dp", "row", "col", None),
            P(None, ("row", "col"), "dp"),
            P(None, ("row", "col"), "dp"),
        ),
        check_vma=False,
    )
```

```python
import functools

import jax
import jax.numpy as jnp
from jax import lax
from jax.experimental import pallas as pl
from jax.experimental.pallas import tpu as pltpu
from jax.sharding import PartitionSpec as P

DILATION_ONE = 64
DILATION_TWO = 128
MESH = pl.DeviceIdType.MESH
F32 = jnp.float32
BF16 = jnp.bfloat16


def passed_along(value, axis, steps):
    count = lax.axis_size(axis)
    first, last = (max(0, -steps), min(count, count - steps))
    return lax.ppermute(value, axis, [(source, source + steps) for source in range(first, last)])


def as_sent(x):

    def short(part):
        return part.astype(jnp.bfloat16) if part.dtype == jnp.float32 else part

    return jax.tree.map(short, x)


def silu_slope(value):
    sigma = jax.nn.sigmoid(value)
    return sigma * (1.0 + value * (1.0 - sigma))


def col_taps(input_grid, offset):
    shifted = []
    for sign_col in (-1, 1):
        if offset < lax.axis_size("col"):
            shifted.append(passed_along(input_grid, "col", -sign_col * offset))
        else:
            shifted.append(jnp.zeros_like(input_grid))
    return jnp.concatenate([shifted[0], input_grid, shifted[1]], axis=3)


def row_data(input_grid, by_tiles):
    if abs(by_tiles) < lax.axis_size("row"):
        return passed_along(as_sent(input_grid), "row", by_tiles).astype(input_grid.dtype)
    return jnp.zeros_like(input_grid)


def apply_dilated_kernel(input_grid, weights, dilation):
    offset = dilation // input_grid.shape[1]
    span_width = weights.shape[1]
    centre = col_taps(input_grid, offset)
    stacks = [row_data(centre, offset), centre, row_data(centre, -offset)]
    partial_terms = [
        jnp.dot(
            stacks[position].reshape(-1, span_width),
            weights[position],
            preferred_element_type=jnp.float32,
        ).astype(jnp.bfloat16)
        for position in range(3)
    ]
    summed = (
        partial_terms[0].astype(jnp.float32)
        + partial_terms[1].astype(jnp.float32)
        + partial_terms[2].astype(jnp.float32)
    )
    return (summed.reshape(input_grid.shape), stacks)


def kernel_weight_gradient(stacks, gradient):
    channels = gradient.shape[-1]
    span_width = 3 * channels
    contract = (((0,), (0,)), ((), ()))
    pieces = []
    flat_grad = gradient.reshape(-1, channels)
    for position in range(3):
        pieces.append(
            lax.dot_general(
                stacks[position].reshape(-1, span_width),
                flat_grad,
                contract,
                preferred_element_type=jnp.float32,
            )
        )
    return jnp.stack(pieces)


def kernel_reversed_taps(weights):
    channels = weights.shape[2]
    return (
        weights.reshape(3, 3, channels, channels)[::-1, ::-1]
        .transpose(0, 1, 3, 2)
        .reshape(3, 3 * channels, channels)
    )


def body(inputs, cotangent, first_kernel, second_kernel):
    first_conv_output, first_tap_stack = apply_dilated_kernel(inputs, first_kernel, DILATION_ONE)
    hidden_activation = (inputs.astype(jnp.float32) + jax.nn.silu(first_conv_output)).astype(
        jnp.bfloat16
    )
    second_conv_output, second_tap_stack = apply_dilated_kernel(
        hidden_activation, second_kernel, DILATION_TWO
    )
    output = (hidden_activation.astype(jnp.float32) + jax.nn.silu(second_conv_output)).astype(
        jnp.bfloat16
    )
    second_upstream_gradient = (
        cotangent.astype(jnp.float32) * silu_slope(second_conv_output)
    ).astype(jnp.bfloat16)
    backward_convolve, ignored_slot = apply_dilated_kernel(
        second_upstream_gradient, kernel_reversed_taps(second_kernel), DILATION_TWO
    )
    grad_second = kernel_weight_gradient(second_tap_stack, second_upstream_gradient)
    grad_middle = (cotangent.astype(jnp.float32) + backward_convolve).astype(jnp.bfloat16)
    first_upstream_gradient = (
        grad_middle.astype(jnp.float32) * silu_slope(first_conv_output)
    ).astype(jnp.bfloat16)
    grad_first = kernel_weight_gradient(first_tap_stack, first_upstream_gradient)
    tiles_summed = (
        lax.psum_scatter(grad_first, ("row", "col"), scatter_dimension=1, tiled=True),
        lax.psum_scatter(grad_second, ("row", "col"), scatter_dimension=1, tiled=True),
    )
    grad_one, grad_two = (
        lax.psum_scatter(tiles_summed[0], "dp", scatter_dimension=2, tiled=True),
        lax.psum_scatter(tiles_summed[1], "dp", scatter_dimension=2, tiled=True),
    )
    return (output, grad_one, grad_two)


def dot(a, b, contract):
    return lax.dot_general(a, b, (contract, ((), ())), preferred_element_type=F32)


def sigmoid(value):
    return 0.5 + 0.5 * jnp.tanh(0.5 * value)


def flipped(index, bits):
    bit = 1
    while bit <= bits:
        if bits & bit:
            index = index + bit - 2 * bit * lax.rem(lax.div(index, bit), 2)
        bit *= 2
    return index


def fused_kernel(
    sizes,
    x_hbm,
    cot_hbm,
    w1_hbm,
    w2_hbm,
    out,
    g1_ref,
    g2_ref,
    x,
    far,
    cot,
    w1,
    w2,
    acc,
    send1,
    recv1,
    send2,
    recv2,
    head_out,
    head_in,
    late_sem,
    told_sem,
    go_sem,
    load_sem,
    far_send,
    far_recv,
    share_send,
    share_recv,
    tile_send,
    tile_recv,
    head_send,
    head_recv,
):
    samples, rows, cols, offset, chunk, heads = sizes
    group = rows * cols
    cells, channels = x.shape
    chunks = cells // chunk
    shares = samples * rows
    share = channels // shares
    piece = 3 * channels // group
    my_dp = lax.axis_index("dp")
    my_row = lax.axis_index("row")
    my_col = lax.axis_index("col")
    me = my_row * cols + my_col
    low = my_col < offset
    partner = jnp.where(low, my_col + offset, my_col - offset)
    tap = jnp.where(low, 2 * channels, 0)
    last_col = offset
    far_end = my_col == last_col

    def is_head(dp, col):
        return functools.reduce(jnp.logical_or, [(dp == a) & (col == b) for a, b in heads])

    head = is_head(my_dp, my_col)

    barrier = pltpu.get_barrier_semaphore()
    tile_peers = []
    for step in reversed(range(1, group)):
        col, row = flipped(my_col, step // rows), flipped(my_row, step % rows)
        tile_peers.append((row * cols + col, {"row": row, "col": col}))
    share_peers = []
    for step in range(samples):
        dp = jnp.where(step < my_dp, step, step + 1) if step < samples - 1 else my_dp
        for turn in reversed(range(rows)):
            row = flipped(my_row, turn)
            if step < samples - 1 or turn:
                share_peers.append((dp * rows + row, {"dp": dp, "row": row}))

    def greet(semaphore, where):
        pl.semaphore_signal(semaphore, inc=1, device_id=where, device_id_type=MESH)

    def greet_plane(semaphore):
        for step in reversed(range(1, shares)):
            dp, row = flipped(my_dp, step // rows), flipped(my_row, step % rows)
            greet(semaphore, {"dp": dp, "row": row})

    front = my_col == 0
    greet(barrier, {"col": partner})

    @pl.when(front)
    def _():
        for col in reversed(range(1, cols)):
            if col != offset:
                greet(barrier, {"col": col})
        if cols == 4:
            for turn in range(1, rows):
                greet(barrier, {"row": flipped(my_row, turn), "col": 1})
        greet_plane(barrier)

    early = jnp.where(front, shares, jnp.where(my_col == offset, 1, 2))
    if cols == 4:
        early = early + jnp.where(my_col == 1, rows - 1, 0)
    loads = [
        pltpu.make_async_copy(x_hbm, x, load_sem.at[0]),
        pltpu.make_async_copy(
            w1_hbm.at[1, pl.ds(channels, channels)], w1.at[pl.ds(0, channels)], load_sem.at[1]
        ),
        pltpu.make_async_copy(
            w1_hbm.at[1, pl.ds(pl.multiple_of(tap, channels), channels)],
            w1.at[pl.ds(channels, channels)],
            load_sem.at[2],
        ),
        pltpu.make_async_copy(w2_hbm.at[1, pl.ds(channels, channels)], w2, load_sem.at[3]),
        pltpu.make_async_copy(cot_hbm, cot, load_sem.at[4]),
    ]
    for load in loads:
        load.start()
    g1_ref[...] = jnp.zeros_like(g1_ref)
    g2_ref[...] = jnp.zeros_like(g2_ref)
    acc[...] = jnp.zeros_like(acc)
    pl.semaphore_wait(barrier, early)

    def exchange(at):
        span = pl.ds(pl.multiple_of(at * chunk, chunk), chunk)
        return pltpu.make_async_remote_copy(
            src_ref=x_hbm.at[span],
            dst_ref=far.at[span],
            send_sem=far_send.at[at],
            recv_sem=far_recv.at[at],
            device_id={"col": partner},
            device_id_type=MESH,
        )

    held = jnp.where(front, chunks - 1, 0) if cols == 4 else 0

    @pl.loop(0, chunks - held)
    def _(at):
        exchange(at).start()

    for load in loads:
        load.wait()

    @pl.when(front)
    def _():
        pl.semaphore_wait(late_sem, cols - 1)
        greet_plane(told_sem)
        pl.semaphore_wait(told_sem, shares - 1)
        for col in reversed(range(1, cols)):
            greet(late_sem, {"col": col})
        if cols == 4:
            pl.semaphore_wait(go_sem, rows)

    @pl.when(jnp.logical_not(front))
    def _():
        greet(late_sem, {"col": 0})

    @pl.loop(chunks - held, chunks)
    def _(at):
        exchange(at).start()

    @pl.loop(0, chunks)
    def _(at):
        exchange(at).wait_recv()

        if cols == 4:

            @pl.when((my_col == 1) & (at == 1))
            def _():
                for row in range(rows):
                    greet(go_sem, {"row": row, "col": 0})

        span = pl.ds(pl.multiple_of(at * chunk, chunk), chunk)
        here = x[span]
        both = jnp.concatenate([here, far[span]], axis=1)
        conv_one = dot(both, w1[...], ((1,), (0,))).astype(BF16).astype(F32)
        sigma_one = sigmoid(conv_one)
        middle = (here.astype(F32) + conv_one * sigma_one).astype(BF16)
        conv_two = dot(middle, w2[...], ((1,), (0,))).astype(BF16).astype(F32)
        sigma_two = sigmoid(conv_two)
        out[span] = (middle.astype(F32) + conv_two * sigma_two).astype(BF16)
        upstream = cot[span].astype(F32)
        delta_two = (upstream * (sigma_two * (1.0 + conv_two * (1.0 - sigma_two)))).astype(BF16)
        back = dot(delta_two, w2[...], ((1,), (1,))).astype(BF16).astype(F32)
        acc[:, 2 * channels :] += dot(delta_two, middle, ((0,), (0,)))
        grad_middle = (upstream + back).astype(BF16).astype(F32)
        delta_one = (grad_middle * (sigma_one * (1.0 + conv_one * (1.0 - sigma_one)))).astype(BF16)
        acc[:, : 2 * channels] += dot(delta_one, both, ((0,), (0,)))

    def packed(total, peer):
        lane = lax.broadcasted_iota(jnp.int32, (total.shape[0], channels), 1)
        start = peer * piece
        shift = lax.rem(3 * channels - start, channels)
        place = start + lane
        back_place = place - piece
        centre = pltpu.roll(total[:, :channels], shift, 1)
        side = pltpu.roll(total[:, channels : 2 * channels], shift, 1)
        second = pltpu.roll(total[:, 2 * channels :], lax.rem(shift + piece, channels), 1)
        one = jnp.where((place >= tap) & (place < tap + channels), side, 0.0)
        one = jnp.where((place >= channels) & (place < 2 * channels), centre, one)
        two = jnp.where((back_place >= channels) & (back_place < 2 * channels), second, 0.0)
        return jnp.where(lane < piece, one, two).astype(BF16)

    mine = my_dp * rows + my_row
    @pl.when(jnp.logical_not(front))
    def _():
        pl.semaphore_wait(late_sem, 1)

    def ahead(at, slot):
        dp, col = heads[at // rows]
        return pltpu.make_async_remote_copy(
            src_ref=head_out.at[at],
            dst_ref=head_in.at[slot],
            send_sem=head_send.at[at],
            recv_sem=head_recv.at[slot],
            device_id={"dp": dp, "row": at % rows, "col": col},
            device_id_type=MESH,
        )

    def send_ahead(ats):
        for at in ats:
            dp, col = heads[at // rows]
            lines = acc[dp * rows * share : (dp + 1) * rows * share, :]
            head_out[at] = packed(lines, at % rows * cols + col)
            ahead(at, mine).start()

    pl.when(far_end)(functools.partial(send_ahead, range(rows)))
    send1[...] = acc[...].astype(BF16).reshape(send1.shape)

    def summed(step, slot):
        peer, where = share_peers[step]
        return pltpu.make_async_remote_copy(
            src_ref=send1.at[peer],
            dst_ref=recv1.at[slot],
            send_sem=share_send.at[step],
            recv_sem=share_recv.at[slot],
            device_id=where,
            device_id_type=MESH,
        )

    for step in range(shares - 1):
        summed(step, mine).start()

    pl.when(far_end)(functools.partial(send_ahead, range(rows, len(heads) * rows)))

    @pl.loop(0, chunks)
    def _(at):
        exchange(at).wait_send()

    total = send1[mine].astype(F32)
    for step in reversed(range(shares - 1)):
        peer = share_peers[step][0]
        summed(step, peer).wait_recv()
        total = total + recv1[peer].astype(F32)

    pieces = []
    for step, (peer, where) in enumerate(tile_peers):
        used = jnp.logical_not(far_end & is_head(my_dp, where["col"]))
        heard = jnp.logical_not(head & (where["col"] == last_col))
        copy = pltpu.make_async_remote_copy(
            src_ref=send2.at[step],
            dst_ref=recv2.at[me],
            send_sem=tile_send.at[step],
            recv_sem=tile_recv.at[step],
            device_id=where,
            device_id_type=MESH,
        )
        send2[step] = packed(total, peer)
        pl.when(used)(copy.start)
        pieces.append((copy, used, heard))
    recv2[me] = packed(total, me)
    for step in range(shares - 1):
        summed(step, mine).wait_send()
    for copy, used, _ in pieces:
        pl.when(used)(copy.wait_send)

    @pl.when(far_end)
    def _():
        for at in range(len(heads) * rows):
            ahead(at, mine).wait_send()

    for copy, _, heard in pieces:
        pl.when(heard)(copy.wait_recv)

    def finish(total, at, size):
        g1_ref[1, pl.ds(at, size)] = total[:, :piece]
        g2_ref[1, pl.ds(at, size)] = total[:, piece : 2 * piece]

    def gathered(part, skip=None):
        used = [recv2[part * cols + col].astype(F32) for col in range(cols) if col != skip]
        return functools.reduce(jnp.add, used)

    @pl.when(jnp.logical_not(head))
    def _():
        for part in range(rows):
            finish(gathered(part), part * share, share)

    @pl.when(head)
    def _():
        total = jnp.concatenate([gathered(part, last_col) for part in range(rows)], axis=0)
        for slot in range(shares):
            ahead(0, slot).wait_recv()
            total = total + head_in[slot].astype(F32)
        finish(total, 0, rows * share)


def store_kernel(count, *refs):
    sems = refs[-1]
    copies = [
        pltpu.make_async_copy(refs[at], refs[count + at], sems.at[at]) for at in range(count)
    ]
    for copy in copies:
        copy.start()
    for copy in copies:
        copy.wait()


def fused_body(sizes, inputs, cotangent, first_kernel, second_kernel):
    samples, rows, cols, offset, chunk, heads = sizes
    group = rows * cols
    channels = inputs.shape[-1]
    shares = samples * rows
    share = channels // shares
    piece = 3 * channels // group
    flat = (inputs.shape[1] * inputs.shape[2], channels)
    hbm = pl.BlockSpec(memory_space=pltpu.HBM)
    vmem = pl.BlockSpec(memory_space=pltpu.VMEM)
    dma = pltpu.SemaphoreType.DMA
    gradient = (3, channels // samples, piece)
    held = pl.pallas_call(
        functools.partial(fused_kernel, sizes),
        out_shape=(pltpu.VMEM(flat, BF16), pltpu.VMEM(gradient, F32), pltpu.VMEM(gradient, F32)),
        in_specs=[hbm] * 4,
        out_specs=(vmem, vmem, vmem),
        scratch_shapes=[
            pltpu.VMEM(flat, BF16),
            pltpu.VMEM(flat, BF16),
            pltpu.VMEM(flat, BF16),
            pltpu.VMEM((2 * channels, channels), BF16),
            pltpu.VMEM((channels, channels), BF16),
            pltpu.VMEM((channels, 3 * channels), F32),
            pltpu.VMEM((shares, share, 3 * channels), BF16),
            pltpu.VMEM((shares, share, 3 * channels), BF16),
            pltpu.VMEM((group - 1, share, channels), BF16),
            pltpu.VMEM((group, share, channels), BF16),
            pltpu.VMEM((len(heads) * rows, rows * share, channels), BF16),
            pltpu.VMEM((shares, rows * share, channels), BF16),
            pltpu.SemaphoreType.REGULAR,
            pltpu.SemaphoreType.REGULAR,
            pltpu.SemaphoreType.REGULAR,
            dma((5,)),
            dma((flat[0] // chunk,)),
            dma((flat[0] // chunk,)),
            dma((shares - 1,)),
            dma((shares,)),
            dma((group - 1,)),
            dma((group - 1,)),
            dma((len(heads) * rows,)),
            dma((shares,)),
        ],
        compiler_params=pltpu.CompilerParams(
            collective_id=0, has_side_effects=True, vmem_limit_bytes=16 * 1024 * 1024
        ),
    )(
        *(
            pltpu.with_memory_space_constraint(part, pltpu.HBM)
            for part in (
                inputs.reshape(flat),
                cotangent.reshape(flat),
                first_kernel,
                second_kernel,
            )
        )
    )
    output, grad_one, grad_two = pl.pallas_call(
        functools.partial(store_kernel, len(held)),
        out_shape=tuple(jax.ShapeDtypeStruct(part.shape, part.dtype) for part in held),
        in_specs=[pl.BlockSpec(memory_space=pl.ANY)] * len(held),
        out_specs=(hbm,) * len(held),
        scratch_shapes=[dma((len(held),))],
        compiler_params=pltpu.CompilerParams(vmem_limit_bytes=1024 * 1024),
    )(*held)
    return (output.reshape(inputs.shape), grad_one.swapaxes(1, 2), grad_two.swapaxes(1, 2))


def either_body(mesh, inputs, cotangent, first_kernel, second_kernel):
    samples, rows, cols = mesh.shape["dp"], mesh.shape["row"], mesh.shape["col"]
    _, height, width, channels = inputs.shape
    offset = DILATION_ONE // width
    piece = 3 * channels // (rows * cols)
    fits = (
        inputs.shape[0] == 1
        and samples > 1
        and all(count & (count - 1) == 0 for count in (samples, rows, cols))
        and DILATION_ONE >= rows * height
        and DILATION_TWO >= rows * height
        and DILATION_TWO >= cols * width
        and DILATION_ONE == offset * width
        and cols == 2 * offset
        and channels % 128 == 0
        and channels % (16 * samples * rows) == 0
        and 3 * channels % (rows * cols) == 0
        and 2 * piece <= channels
        and (height * width) % (2 * channels) == 0
        and height * width >= 4 * channels
    )
    if not fits:
        return body(inputs, cotangent, first_kernel, second_kernel)
    heads = [(0, 0)] + [(dp, 0) for dp in range(1, samples - 1)]
    if cols > 2:
        heads.append((0, 1))
    sizes = (samples, rows, cols, offset, 2 * channels, heads)
    return fused_body(sizes, inputs, cotangent, first_kernel, second_kernel)


def solution(mesh):
    placed = (P("dp", "row", "col", None), P("dp", "row", "col", None), P(), P())
    return jax.shard_map(
        functools.partial(either_body, mesh),
        mesh=mesh,
        in_specs=placed,
        out_specs=(
            P("dp", "row", "col", None),
            P(None, ("row", "col"), "dp"),
            P(None, ("row", "col"), "dp"),
        ),
        check_vma=False,
    )
```
